768 devices in a mesh: dp: 64 (over y, z_lo, core), tensor: 12 (over x, z_hi).
Axes of the slice: x: 4, y: 8, z: 12 (z_hi: 3, z_lo: 4; z = z_hi * 4 + z_lo), core: 2. Of those that a mesh axis runs over, the one named last changes fastest.
Arguments:
- latent: bfloat16 [36864, 512], P('dp'), may hold values from -6 to 6
- q_nope: bfloat16 [36864, 6144], P('dp', 'tensor'), may hold values from -6 to 6
- q_rope: bfloat16 [36864, 3072], P('dp', 'tensor'), may hold values from -40 to 40
- k_rope: bfloat16 [36864, 64], P('dp'), may hold values from -4.5 to 4.5
- grad_out: bfloat16 [36864, 6144], P('dp', 'tensor'), may hold values from -6 to 6
- offsets: int32 [64], P('dp'), may hold values from 1 to 575
- weight: bfloat16 [256, 48, 512], P(None, 'tensor'), may hold values from -0.25 to 0.25
- basis: float32 [512, 512], replicated, may hold values from -1 to 1
- first_moment: float32 [256, 48, 512], P('dp', 'tensor'), may hold values from -30 to 30
- second_rot: float32 [256, 48, 512], P('dp', 'tensor'), may hold values from 1 to 400
- second_plain: float32 [256, 48, 512], P('dp', 'tensor'), may hold values from 1 to 400
Outputs:
- grad_latent: bfloat16 [36864, 512], P(('dp', 'tensor'))
- new_weight: bfloat16 [256, 48, 512], P(None, 'tensor')
- new_first: float32 [256, 48, 512], P('dp', 'tensor')
- new_second: float32 [256, 48, 512], P('dp', 'tensor')
- new_plain: float32 [256, 48, 512], P('dp', 'tensor')
The draws below stay inside these ranges and needn't reach their ends.
All inputs are finite; a program needn't handle non-finite values.
Results may differ from the reference program's by a relative error of at most 0.011.
Values may be sent and summed in bfloat16 or wider, within the bound.
A program may use at most 64 MiB of HBM per device.

```python
import math
import jax
import jax.numpy as jnp
from jax import lax

LAT = 512
HD = 128
ROPE = 64
SEQ = 576
HEADS = 48
GROUPS = 64
TOKENS = 36864


def rope_pair(key):
    key_query = jax.random.fold_in(key, 11)
    key_keys = jax.random.fold_in(key, 12)
    key_rope = jnp.clip(jax.random.normal(key_keys, (GROUPS, SEQ, ROPE), jnp.float32), -4.5, 4.5)
    query_rope = jnp.clip(jax.random.normal(key_query, (GROUPS, SEQ, HEADS, ROPE), jnp.float32), -6.0, 6.0)
    return (query_rope.reshape(GROUPS * SEQ, HEADS * ROPE), key_rope.reshape(GROUPS * SEQ, ROPE))


def draw_q_rope(key, part):
    return rope_pair(key)[0].astype(jnp.bfloat16)


def draw_k_rope(key, part):
    return rope_pair(key)[1].astype(jnp.bfloat16)


def draw_basis(key, part):
    highest = lax.Precision.HIGHEST
    jitter_terms = jax.random.normal(jax.random.fold_in(key, 21), (LAT, LAT), jnp.float32) * (0.6 / LAT ** 0.5)
    matrix = (jnp.eye(LAT, dtype=jnp.float32) + jitter_terms) / 1.7
    for _ in range(16):
        square = jnp.dot(matrix, matrix.T, precision=highest)
        matrix = 1.5 * matrix - 0.5 * jnp.dot(square, matrix, precision=highest)
    return jnp.clip(matrix, -1.0, 1.0)


def place_ends(values, stream_key, low, high):
    dims = values.shape
    index_at = [jax.random.randint(jax.random.fold_in(stream_key, axis), (), 0, dims[axis]) for axis in range(len(dims))]
    values = values.at[tuple(index_at)].set(low)
    longest = dims.index(max(dims))
    index_at[longest] = (index_at[longest] + 1) % dims[longest]
    return values.at[tuple(index_at)].set(high)


def steps_of(own_key, extent, split, least, top_value):
    loudness = 1.0
    for dim, blocks in split:
        steps = jax.random.uniform(jax.random.fold_in(jax.random.fold_in(own_key, 6), dim), (blocks,), jnp.float32, least / len(split), top_value / len(split))
        loudness = loudness * jnp.repeat(jnp.exp(steps), extent[dim] // blocks).reshape((-1,) + (1,) * (len(extent) - 1 - dim))
    return loudness


def noise(rng, dims, scale, limit, split=(), kind=jnp.bfloat16):
    values = scale * jax.random.normal(rng, dims, jnp.float32)
    if split:
        values = values * steps_of(rng, dims, split, -0.22, 0.18)
    return jnp.clip(values, -limit, limit).astype(kind)


def setup_inputs(seed: int = 0) -> dict:
    key_of = jax.random.split(jax.random.key(seed), 12)
    return {
        "latent": noise(key_of[0], (TOKENS, LAT), 1.0, 6.0, ((0, 64),)),
        "q_nope": noise(key_of[1], (TOKENS, HEADS * HD), 1.0, 6.0, ((0, 64), (1, 12))),
        "q_rope": draw_q_rope(jax.random.fold_in(key_of[11], 71), 0),
        "k_rope": draw_k_rope(jax.random.fold_in(key_of[11], 71), 0),
        "grad_out": noise(key_of[4], (TOKENS, HEADS * HD), 1.0, 6.0, ((0, 64), (1, 12))),
        "offsets": place_ends(jax.random.randint(key_of[5], (GROUPS,), 1, SEQ), jax.random.fold_in(key_of[5], 1), 1, SEQ - 1).astype(jnp.int32),
        "weight": noise(key_of[6], (2 * HD, HEADS, LAT), LAT ** -0.5, 0.25, ((1, 12),)),
        "basis": draw_basis(jax.random.fold_in(key_of[11], 71), 0),
        "first_moment": noise(key_of[8], (2 * HD, HEADS, LAT), 5.0, 30.0, ((0, 64), (1, 12)), jnp.float32),
        "second_rot": jnp.clip(jnp.exp(math.log(400.0) - 5.9914645 * jax.random.uniform(key_of[9], (2 * HD, HEADS, LAT), jnp.float32) ** steps_of(key_of[9], (2 * HD, HEADS, LAT), ((0, 64), (1, 12)), -0.2, 0.2)), 1.0, 400.0),
        "second_plain": jnp.clip(jnp.exp(math.log(400.0) - 5.9914645 * jax.random.uniform(key_of[10], (2 * HD, HEADS, LAT), jnp.float32) ** steps_of(key_of[10], (2 * HD, HEADS, LAT), ((0, 64), (1, 12)), -0.2, 0.2)), 1.0, 400.0),
    }


beta_first = 0.9
beta_second = 0.95
epsilon = 1e-08
learn_rate = 0.002
decay_rate = 0.1
blend_share = 0.5

def group_pass(weight, latent, q_nope, q_rope, k_rope, grad_out, offset):
    f32 = jnp.float32
    score_scale = float(HD + ROPE) ** (-0.5)
    key_value = jnp.einsum('tc,rhc->thr', latent.astype(f32), weight.astype(f32)).astype(jnp.bfloat16)
    keys = key_value[:, :, :HD].astype(f32)
    values = key_value[:, :, HD:].astype(f32)
    query_main = q_nope.reshape(SEQ, HEADS, HD).astype(f32)
    query_side = q_rope.reshape(SEQ, HEADS, ROPE).astype(f32)
    out_grads = grad_out.reshape(SEQ, HEADS, HD).astype(f32)
    scores = (jnp.einsum('ihd,jhd->hij', query_main, keys) + jnp.einsum('ihe,je->hij', query_side, k_rope.astype(f32))) * score_scale
    positions = jnp.arange(SEQ, dtype=jnp.int32)
    visible = positions[None, :] <= jnp.maximum(positions[:, None], offset - 1)
    masked = jnp.where(visible[None], scores, -jnp.inf)
    row_max = lax.optimization_barrier(jnp.max(masked, axis=-1, keepdims=True))
    exp_terms = jnp.where(visible[None], jnp.exp(masked - row_max), 0.0)
    attn_probs = exp_terms / lax.optimization_barrier(jnp.sum(exp_terms, axis=-1, keepdims=True))
    probs_low = attn_probs.astype(jnp.bfloat16).astype(f32)
    attended = jnp.einsum('hij,jhd->ihd', probs_low, values)
    row_delta = lax.optimization_barrier(jnp.sum(out_grads * attended, axis=-1))
    grad_probs = jnp.einsum('ihd,jhd->hij', out_grads, values)
    grad_scores = (attn_probs * (grad_probs - jnp.transpose(row_delta)[:, :, None]) * score_scale).astype(jnp.bfloat16).astype(f32)
    grad_keys = jnp.einsum('hij,ihd->jhd', grad_scores, query_main)
    grad_values = jnp.einsum('hij,ihd->jhd', probs_low, out_grads)
    grad_kv = jnp.concatenate([grad_keys, grad_values], axis=-1).astype(jnp.bfloat16).astype(f32)
    grad_latent = jnp.einsum('thr,rhc->tc', grad_kv, weight.astype(f32)).astype(jnp.bfloat16)
    weight_part = jnp.einsum('thr,tc->rhc', grad_kv, latent.astype(f32))
    return (grad_latent, weight_part)

def reference(latent, q_nope, q_rope, k_rope, grad_out, offsets, weight, basis, first_moment, second_rot, second_plain):
    f32 = jnp.float32
    highest = lax.Precision.HIGHEST
    stacked = (latent.reshape(GROUPS, SEQ, LAT), q_nope.reshape(GROUPS, SEQ, HEADS * HD), q_rope.reshape(GROUPS, SEQ, HEADS * ROPE), k_rope.reshape(GROUPS, SEQ, ROPE), grad_out.reshape(GROUPS, SEQ, HEADS * HD), offsets)

    def step_group(carry, inputs):
        grad_latent, weight_part = group_pass(weight, inputs[0], inputs[1], inputs[2], inputs[3], inputs[4], inputs[5])
        return (carry + weight_part, grad_latent)
    weight_grad, latent_parts = lax.scan(step_group, jnp.zeros((2 * HD, HEADS, LAT), f32), stacked)
    grad_latent = latent_parts.reshape(TOKENS, LAT)
    rotated = jnp.einsum('rhc,ce->rhe', weight_grad, basis, precision=highest)
    new_first = beta_first * first_moment + (1.0 - beta_first) * rotated
    new_second = beta_second * second_rot + (1.0 - beta_second) * rotated * rotated
    new_plain = beta_second * second_plain + (1.0 - beta_second) * weight_grad * weight_grad
    soap_part = jnp.einsum('rhe,ce->rhc', new_first / (jnp.sqrt(new_second) + epsilon), basis, precision=highest)
    back_moment = jnp.einsum('rhe,ce->rhc', new_first, basis, precision=highest)
    direction = blend_share * soap_part + blend_share * back_moment / (jnp.sqrt(new_plain) + epsilon)
    old_weight = weight.astype(f32)
    new_weight = (old_weight - learn_rate * (direction + decay_rate * old_weight)).astype(jnp.bfloat16)
    return (grad_latent, new_weight, new_first, new_second, new_plain)
```

```python
import functools
import math

import jax
import jax.numpy as jnp
from jax import lax
from jax.experimental import pallas as pl
from jax.experimental.pallas import tpu as pltpu
from jax.sharding import PartitionSpec as P

beta_first = 0.9
beta_second = 0.95
epsilon = 1e-08
learn_rate = 0.002
decay_rate = 0.1
blend_share = 0.5

NY, NZ, NC = 8, 4, 2
NX, NH = 4, 3
f32 = jnp.float32
bf16 = jnp.bfloat16

NN = (((1,), (0,)), ((), ()))
NT = (((1,), (1,)), ((), ()))


def mm(a, b, dims=NN):
    return lax.dot_general(a, b, dims, preferred_element_type=f32)


def iota(shape, dim):
    return lax.broadcasted_iota(jnp.int32, shape, dim)


def one_hot_rows(source, columns):
    return jnp.where(source == iota((source.shape[0], columns), 1), 1.0, 0.0).astype(bf16)


def split(x):
    high = x.astype(bf16)
    return high, (x - high.astype(f32)).astype(bf16)


def kernel(
    off, lat, qn, qr, kr, go, w, basis, fm, sr, sp,
    gl_out, gw, nf_out, ns_out, np_out,
    krp, gkv, pts, gss, wg_own, wg_send, c_recv, y_send, y_recv, zsrc, z_send, z_recv,
    gl_send, x_recv, zh_send, zh_recv, b_hi, b_lo, t_fm, t_sr, t_sp,
    c_ss, c_rs, y_ss, y_rs, z_ss, z_rs, x_ss, x_rs, h_ss, h_rs,
    a1_ss, a1_rs, b1_ss, b1_rs, a2_ss, a2_rs, b2_ss, b2_rs, ga_ss, ga_rs, gb_ss, gb_rs,
):
    seq, _ = lat.shape
    heads, rows, latw = w.shape
    hd = rows // 2
    half = latw // 2
    dp = lax.axis_index("dp")
    tn = lax.axis_index("tensor")
    my_y, my_z, my_c = dp // (NZ * NC), (dp // NC) % NZ, dp % NC
    my_x, my_h = tn // NH, tn % NH

    def at_y(k):
        return (((my_y + k) % NY) * (NZ * NC) + my_z * NC + my_c, tn)

    def at_z(k):
        return (my_y * (NZ * NC) + ((my_z + k) % NZ) * NC + my_c, tn)

    def at_x(k):
        return (dp, ((my_x + k) % NX) * NH + my_h)

    def at_h(k):
        return (dp, my_x * NH + (my_h + k) % NH)

    partner = (my_y * (NZ * NC) + my_z * NC + (1 - my_c), tn)

    def remote(src, dst, ss, rs, to):
        return pltpu.make_async_remote_copy(
            src_ref=src, dst_ref=dst, send_sem=ss, recv_sem=rs,
            device_id=to, device_id_type=pl.DeviceIdType.MESH,
        )

    barrier = pltpu.get_barrier_semaphore()
    greet = (
        [partner]
        + [at_y(k) for k in range(1, NY)]
        + [at_z(k) for k in range(1, NZ)]
        + [at_x(k) for k in range(1, NX)]
        + [at_h(k) for k in range(1, NH)]
    )
    for to in greet:
        pl.semaphore_signal(barrier, inc=1, device_id=to, device_id_type=pl.DeviceIdType.MESH)

    sent = []

    lane = iota((kr.shape[1], 2 * kr.shape[1]), 1)
    row = iota((kr.shape[1], 2 * kr.shape[1]), 0)
    for odd in range(2):
        place = jnp.where(lane == row + odd * kr.shape[1], 1.0, 0.0).astype(bf16)
        krp[odd] = mm(kr[...], place).astype(bf16)

    o = iota((rows, 1), 0)
    src_row = (
        ((o >> 4) & 7) * 32 + ((o >> 2) & 3) * 8 + jnp.where((o >> 7) == 0, my_c, 1 - my_c) * 4 + (o & 3)
    )
    perm = one_hot_rows(src_row, rows)

    scale = float(hd + kr.shape[1]) ** (-0.5)
    to_exp2 = scale * math.log2(math.e)
    last_seen = off[0] - 1
    blocks = [(0, 256), (256, 256), (512, seq - 512)]

    def core_copy(h):
        return remote(wg_send.at[h], c_recv.at[h], c_ss.at[h], c_rs.at[h], partner)

    def y_copy(h, k):
        return remote(
            y_send.at[h, (my_y + k) % NY], y_recv.at[h, k - 1],
            y_ss.at[h, k - 1], y_rs.at[h, k - 1], at_y(k),
        )

    def finish_core(h):
        copy = core_copy(h)
        copy.wait_recv()
        both = wg_own[h] + c_recv[h].astype(f32)
        y_send[h] = both.astype(bf16).reshape(NY, rows // 16, latw)
        for k in (4, 3, 5, 2, 6, 1, 7):
            c = y_copy(h, k)
            c.start()
            sent.append(c)

    for h in range(heads):
        lanes = slice(h * hd, (h + 1) * hd)
        pair = slice((h // 2) * hd, (h // 2 + 1) * hd)
        kv = mm(lat[...], w[h], NT).astype(bf16)
        key = jnp.concatenate([kv[:, :hd], krp[h % 2]], axis=1)
        value = kv[:, hd:]
        buf = h % 2
        for start, size in blocks:
            at = slice(start, start + size)
            query = jnp.concatenate([qn[at, lanes], qr[at, pair]], axis=1)
            scores = mm(key, query, NT)
            limit = jnp.maximum(iota((1, size), 1) + start, last_seen)
            seen = iota((seq, size), 0) <= limit
            masked = jnp.where(seen, scores, -jnp.inf)
            top = jnp.max(masked, axis=0, keepdims=True)
            terms = jnp.exp2((masked - top) * to_exp2)
            probs = terms * (1.0 / jnp.sum(terms, axis=0, keepdims=True))
            low = probs.astype(bf16)
            pts[buf, :, at] = low
            grad_probs = mm(value, go[at, lanes], NT)
            delta = jnp.sum(low.astype(f32) * grad_probs, axis=0, keepdims=True)
            gss[buf, :, at] = (probs * (grad_probs - delta) * scale).astype(bf16)
        grad_keys = mm(gss[buf], qn[:, lanes])
        grad_values = mm(pts[buf], go[:, lanes])
        both = jnp.concatenate([grad_keys.astype(bf16), grad_values.astype(bf16)], axis=1)
        gkv[h] = both
        turned = mm(perm, both, NT).astype(bf16)
        part = mm(turned, lat[...])
        wg_own[h] = part[: rows // 2]
        wg_send[h] = part[rows // 2 :].astype(bf16)
        if h == 0:
            pl.semaphore_wait(barrier, len(greet))
        c = core_copy(h)
        c.start()
        sent.append(c)
        if h > 0:
            finish_core(h - 1)

    share = seq // NX
    for xb in range(NX):
        at = slice(xb * share, (xb + 1) * share)
        total = mm(gkv[0, at], w[0])
        for h in range(1, heads):
            total = total + mm(gkv[h, at], w[h])
        gl_send[xb] = total.astype(bf16)

    finish_core(heads - 1)

    def x_copy(k):
        return remote(
            gl_send.at[(my_x + k) % NX], x_recv.at[k - 1], x_ss.at[k - 1], x_rs.at[k - 1], at_x(k)
        )

    for k in (2, 1, 3):
        c = x_copy(k)
        c.start()
        sent.append(c)

    high, low = split(basis[...])
    b_hi[...] = high
    b_lo[...] = low
    per = rows // (NY * NZ * NC)
    for i in range(per):
        at = slice(i * heads, (i + 1) * heads)
        t_fm[at] = fm[i]
        t_sr[at] = sr[i]
        t_sp[at] = sp[i]
    near = pl.multiple_of((dp // 4) * 16, 16)
    o = iota((16, 1), 0)
    old = jnp.zeros((16, latw), f32)
    for h in range(heads):
        pick = jnp.where((o & 3) == h, (dp % 4) * 4 + (o >> 2), -1)
        old = old + mm(one_hot_rows(pick, 16), w[h, pl.ds(near, 16), :])

    for h in range(heads):
        total = y_send[h, my_y].astype(f32)
        for k in range(1, NY):
            y_copy(h, k).wait_recv()
            total = total + y_recv[h, k - 1].astype(f32)
        zsrc[h * 16 : (h + 1) * 16] = total.astype(bf16)
    o = iota((heads * 16, 1), 0)
    order = one_hot_rows((o & 3) * 16 + (o >> 4) * 4 + ((o >> 2) & 3), heads * 16)
    z_send[...] = mm(order, zsrc[...]).astype(bf16).reshape(NZ, 16, latw)

    def z_copy(k):
        return remote(
            z_send.at[(my_z + k) % NZ], z_recv.at[k - 1], z_ss.at[k - 1], z_rs.at[k - 1], at_z(k)
        )

    for k in range(1, NZ):
        c = z_copy(k)
        c.start()
        sent.append(c)

    total = gl_send[my_x].astype(f32)
    for k in range(1, NX):
        x_copy(k).wait_recv()
        total = total + x_recv[k - 1].astype(f32)
    zh_send[...] = total.astype(bf16).reshape(NH, share // NH, latw)

    def h_copy(k):
        return remote(
            zh_send.at[(my_h + k) % NH], zh_recv.at[k - 1], h_ss.at[k - 1], h_rs.at[k - 1], at_h(k)
        )

    for k in range(1, NH):
        c = h_copy(k)
        c.start()
        sent.append(c)

    grad = z_send[my_z].astype(f32)
    for k in range(1, NZ):
        z_copy(k).wait_recv()
        grad = grad + z_recv[k - 1].astype(f32)

    g_hi, g_lo = split(grad)
    rotated = mm(g_hi, b_hi[...]) + mm(g_lo, b_hi[...]) + mm(g_hi, b_lo[...])
    first = beta_first * t_fm[...] + (1.0 - beta_first) * rotated
    second = beta_second * t_sr[...] + (1.0 - beta_second) * rotated * rotated
    plain = beta_second * t_sp[...] + (1.0 - beta_second) * grad * grad
    stacked = jnp.concatenate([first / (jnp.sqrt(second) + epsilon), first], axis=0)
    s_hi, s_lo = split(stacked)
    back = mm(s_hi, b_hi[...], NT) + mm(s_lo, b_hi[...], NT) + mm(s_hi, b_lo[...], NT)
    direction = blend_share * back[:16] + blend_share * back[16:] / (jnp.sqrt(plain) + epsilon)
    new = (old - learn_rate * (direction + decay_rate * old)).astype(bf16)
    gw[my_y, my_z, my_c] = new

    lo, hi = slice(0, half), slice(half, latw)

    def a1(k):
        ref = gw.at[my_y, my_z, my_c, :, lo]
        return remote(ref, ref, a1_ss.at[k - 1], a1_rs.at[k - 1], at_z(k))

    def b1(k):
        ref = gw.at[my_y, my_z, my_c, :, hi]
        return remote(ref, ref, b1_ss.at[k - 1], b1_rs.at[k - 1], at_y(k))

    def a2(k):
        ref = gw.at[my_y, :, my_c, :, lo]
        return remote(ref, ref, a2_ss.at[k - 1], a2_rs.at[k - 1], at_y(k))

    def b2(k):
        ref = gw.at[:, my_z, my_c, :, hi]
        return remote(ref, ref, b2_ss.at[k - 1], b2_rs.at[k - 1], at_z(k))

    def ga(k):
        ref = gw.at[(my_y + NY - k) % NY, :, my_c, :, lo]
        return remote(ref, ref, ga_ss.at[k], ga_rs.at[k], partner)

    def gb(k):
        ref = gw.at[:, (my_z + NZ - k) % NZ, my_c, :, hi]
        return remote(ref, ref, gb_ss.at[k], gb_rs.at[k], partner)

    def go_on(c):
        c.start()
        sent.append(c)

    for k in (1, 2, 3):
        go_on(a1(k))
    for k in (4, 3, 5, 2, 6, 1, 7):
        go_on(b1(k))

    for i in range(per):
        at = slice(i * heads, (i + 1) * heads)
        nf_out[i] = first[at]
        ns_out[i] = second[at]
        np_out[i] = plain[at]

    for k in (1, 2, 3):
        a1(k).wait_recv()
    for k in (4, 3, 5, 2, 6, 1, 7):
        go_on(a2(k))
    for k in range(1, NY):
        b1(k).wait_recv()
    for k in (3, 2, 1):
        go_on(b2(k))
    go_on(ga(0))
    go_on(gb(0))

    total = zh_send[my_h].astype(f32)
    for k in range(1, NH):
        h_copy(k).wait_recv()
        total = total + zh_recv[k - 1].astype(f32)
    gl_out[...] = total.astype(bf16)

    for k in (1, 7, 2, 6, 3, 5, 4):
        a2(k).wait_recv()
        go_on(ga(k))
    for k in (1, 2, 3):
        b2(k).wait_recv()
        go_on(gb(k))
    for k in range(NY):
        ga(k).wait_recv()
    for k in range(NZ):
        gb(k).wait_recv()
    for c in sent:
        c.wait_send()


def local(
    latent, q_nope, q_rope, k_rope, grad_out, offsets, weight, basis,
    first_moment, second_rot, second_plain,
):
    seq, latw = latent.shape
    rows, heads, _ = weight.shape
    per = first_moment.shape[0]
    by_head = jnp.transpose(weight, (1, 0, 2))
    vmem = pl.BlockSpec(memory_space=pltpu.VMEM)
    dma = pltpu.SemaphoreType.DMA
    V = pltpu.VMEM
    share = seq // NX
    outs = pl.pallas_call(
        kernel,
        out_shape=(
            jax.ShapeDtypeStruct((share // NH, latw), bf16),
            jax.ShapeDtypeStruct((NY, NZ, NC, per * heads, latw), bf16),
            jax.ShapeDtypeStruct((per, heads, latw), f32),
            jax.ShapeDtypeStruct((per, heads, latw), f32),
            jax.ShapeDtypeStruct((per, heads, latw), f32),
        ),
        in_specs=[pl.BlockSpec(memory_space=pltpu.SMEM)] + [vmem] * 10,
        out_specs=[vmem] * 5,
        scratch_shapes=[
            V((2, seq, 128), bf16),
            V((heads, seq, rows), bf16),
            V((2, seq, seq), bf16),
            V((2, seq, seq), bf16),
            V((heads, rows // 2, latw), f32),
            V((heads, rows // 2, latw), bf16),
            V((heads, rows // 2, latw), bf16),
            V((heads, NY, 16, latw), bf16),
            V((heads, NY - 1, 16, latw), bf16),
            V((heads * 16, latw), bf16),
            V((NZ, 16, latw), bf16),
            V((NZ - 1, 16, latw), bf16),
            V((NX, share, latw), bf16),
            V((NX - 1, share, latw), bf16),
            V((NH, share // NH, latw), bf16),
            V((NH - 1, share // NH, latw), bf16),
            V((latw, latw), bf16),
            V((latw, latw), bf16),
            V((16, latw), f32),
            V((16, latw), f32),
            V((16, latw), f32),
            dma((heads,)), dma((heads,)),
            dma((heads, NY - 1)), dma((heads, NY - 1)),
            dma((NZ - 1,)), dma((NZ - 1,)),
            dma((NX - 1,)), dma((NX - 1,)),
            dma((NH - 1,)), dma((NH - 1,)),
            dma((NZ - 1,)), dma((NZ - 1,)),
            dma((NY - 1,)), dma((NY - 1,)),
            dma((NY - 1,)), dma((NY - 1,)),
            dma((NZ - 1,)), dma((NZ - 1,)),
            dma((NY,)), dma((NY,)),
            dma((NZ,)), dma((NZ,)),
        ],
        compiler_params=pltpu.CompilerParams(
            collective_id=0, has_side_effects=True, vmem_limit_bytes=60 * 2**20
        ),
    )(
        offsets, latent, q_nope, q_rope, k_rope, grad_out, by_head, basis,
        first_moment, second_rot, second_plain,
    )
    grad_latent, gathered, moment, rotated_sq, plain_sq = outs
    return (grad_latent, gathered.reshape(rows, heads, latw), moment, rotated_sq, plain_sq)


def solution(mesh):
    return jax.shard_map(
        local,
        mesh=mesh,
        in_specs=(
            P("dp", None),
            P("dp", "tensor"),
            P("dp", "tensor"),
            P("dp", None),
            P("dp", "tensor"),
            P("dp"),
            P(None, "tensor", None),
            P(),
            P("dp", "tensor", None),
            P("dp", "tensor", None),
            P("dp", "tensor", None),
        ),
        out_specs=(
            P(("dp", "tensor"), None),
            P(None, "tensor", None),
            P("dp", "tensor", None),
            P("dp", "tensor", None),
            P("dp", "tensor", None),
        ),
        check_vma=False,
    )
```

```python
import functools
import math

import jax
import jax.numpy as jnp
from jax import lax
from jax.experimental import pallas as pl
from jax.experimental.pallas import tpu as pltpu
from jax.sharding import PartitionSpec as P

beta_first = 0.9
beta_second = 0.95
epsilon = 1e-08
learn_rate = 0.002
decay_rate = 0.1
blend_share = 0.5

NY, NZ, NC = 8, 4, 2
NX, NH = 4, 3
f32 = jnp.float32
bf16 = jnp.bfloat16

NN = (((1,), (0,)), ((), ()))
NT = (((1,), (1,)), ((), ()))
TN = (((0,), (0,)), ((), ()))


def mm(a, b, dims=NN):
    return lax.dot_general(a, b, dims, preferred_element_type=f32)


def iota(shape, dim):
    return lax.broadcasted_iota(jnp.int32, shape, dim)


def one_hot_rows(source, columns):
    return jnp.where(source == iota((source.shape[0], columns), 1), 1.0, 0.0).astype(bf16)


def split(x):
    high = x.astype(bf16)
    return high, (x - high.astype(f32)).astype(bf16)


def kernel(
    off, lat, qn, qr, kr, go, w, basis, fm, sr, sp,
    gl_out, gw, nf_out, ns_out, np_out,
    krp, gkv, pts, gss, wg_own, wg_send, c_recv, y_send, y_recv, z_send, z_recv,
    asrc, bsrc, za_send, za_recv, yb_send, yb_recv,
    gl_send, x_recv, zh_send, zh_recv, b_hi, b_lo, t_fm, t_sr, t_sp,
    c_ss, c_rs, y_ss, y_rs, z_ss, z_rs, za_ss, za_rs, yb_ss, yb_rs, x_ss, x_rs, h_ss, h_rs,
    a1_ss, a1_rs, b1_ss, b1_rs, a2_ss, a2_rs, b2_ss, b2_rs, ga_ss, ga_rs, gb_ss, gb_rs,
):
    seq, _ = lat.shape
    heads, rows, latw = w.shape
    hd = rows // 2
    half = latw // 2
    dp = lax.axis_index("dp")
    tn = lax.axis_index("tensor")
    my_y, my_z, my_c = dp // (NZ * NC), (dp // NC) % NZ, dp % NC
    my_x, my_h = tn // NH, tn % NH

    def at_y(k):
        return (((my_y + k) % NY) * (NZ * NC) + my_z * NC + my_c, tn)

    def at_z(k):
        return (my_y * (NZ * NC) + ((my_z + k) % NZ) * NC + my_c, tn)

    def at_x(k):
        return (dp, ((my_x + k) % NX) * NH + my_h)

    def at_h(k):
        return (dp, my_x * NH + (my_h + k) % NH)

    partner = (my_y * (NZ * NC) + my_z * NC + (1 - my_c), tn)

    def remote(src, dst, ss, rs, to):
        return pltpu.make_async_remote_copy(
            src_ref=src, dst_ref=dst, send_sem=ss, recv_sem=rs,
            device_id=to, device_id_type=pl.DeviceIdType.MESH,
        )

    barrier = pltpu.get_barrier_semaphore()
    greet = (
        [partner]
        + [at_y(k) for k in range(1, NY)]
        + [at_z(k) for k in range(1, NZ)]
        + [at_x(k) for k in range(1, NX)]
        + [at_h(k) for k in range(1, NH)]
    )
    for to in greet:
        pl.semaphore_signal(barrier, inc=1, device_id=to, device_id_type=pl.DeviceIdType.MESH)

    sent = []

    rope = kr.shape[0]
    lane = iota((rope, 2 * rope), 1)
    row = iota((rope, 2 * rope), 0)
    for odd in range(2):
        place = jnp.where(lane == row + odd * rope, 1.0, 0.0).astype(bf16)
        krp[odd] = mm(kr[...], place, TN).astype(bf16)

    o = iota((rows, 1), 0)
    core_i = jnp.where((o >> 7) == 0, my_c, 1 - my_c) * 4 + (o & 3)
    perm_a = one_hot_rows(((o >> 4) & 7) * 32 + ((o >> 2) & 3) * 8 + core_i, rows)
    perm_b = one_hot_rows(((o >> 2) & 7) * 32 + ((o >> 5) & 3) * 8 + core_i, rows)

    scale = float(hd + rope) ** (-0.5)
    to_exp2 = scale * math.log2(math.e)
    last_seen = off[0] - 1
    blocks = [(0, 256), (256, 256), (512, seq - 512)]

    def core_copy(h):
        return remote(wg_send.at[h], c_recv.at[h], c_ss.at[h], c_rs.at[h], partner)

    def y_copy(h, k):
        return remote(
            y_send.at[h, (my_y + k) % NY], y_recv.at[h, k - 1],
            y_ss.at[h, k - 1], y_rs.at[h, k - 1], at_y(k),
        )

    def z_copy(h, k):
        return remote(
            z_send.at[h, (my_z + k) % NZ], z_recv.at[h, k - 1],
            z_ss.at[h, k - 1], z_rs.at[h, k - 1], at_z(k),
        )

    def go_on(c):
        c.start()
        sent.append(c)

    def finish_core(h):
        core_copy(h).wait_recv()
        both = (wg_own[h, 0] + c_recv[h, 0].astype(f32)).astype(bf16)
        y_send[h] = both.reshape(NY, 16, half)
        both = (wg_own[h, 1] + c_recv[h, 1].astype(f32)).astype(bf16)
        z_send[h] = both.reshape(NZ, 32, half)
        for k in (4, 3, 5, 2, 6, 1, 7):
            go_on(y_copy(h, k))
        for k in (2, 1, 3):
            go_on(z_copy(h, k))

    for h in range(heads):
        lanes = slice(h * hd, (h + 1) * hd)
        pair = slice((h // 2) * hd, (h // 2 + 1) * hd)
        kv = mm(lat[...], w[h], NT).astype(bf16)
        key = jnp.concatenate([kv[:, :hd], krp[h % 2]], axis=1)
        value = kv[:, hd:]
        buf = h % 2
        for start, size in blocks:
            at = slice(start, start + size)
            query = jnp.concatenate([qn[at, lanes], qr[at, pair]], axis=1)
            scores = mm(key, query, NT)
            limit = jnp.maximum(iota((1, size), 1) + start, last_seen)
            seen = iota((seq, size), 0) <= limit
            masked = jnp.where(seen, scores, -jnp.inf)
            top = jnp.max(masked, axis=0, keepdims=True)
            terms = jnp.exp2((masked - top) * to_exp2)
            probs = terms * (1.0 / jnp.sum(terms, axis=0, keepdims=True))
            low = probs.astype(bf16)
            pts[buf, :, at] = low
            grad_probs = mm(value, go[at, lanes], NT)
            delta = jnp.sum(low.astype(f32) * grad_probs, axis=0, keepdims=True)
            gss[buf, :, at] = (probs * (grad_probs - delta) * scale).astype(bf16)
        grad_keys = mm(gss[buf], qn[:, lanes])
        grad_values = mm(pts[buf], go[:, lanes])
        both = jnp.concatenate([grad_keys.astype(bf16), grad_values.astype(bf16)], axis=1)
        gkv[h] = both
        for side, perm in ((0, perm_a), (1, perm_b)):
            turned = mm(perm, both, NT).astype(bf16)
            part = mm(turned, lat[:, side * half : (side + 1) * half])
            wg_own[h, side] = part[: rows // 2]
            wg_send[h, side] = part[rows // 2 :].astype(bf16)
        if h == 0:
            pl.semaphore_wait(barrier, len(greet))
        c = core_copy(h)
        c.start()
        sent.append(c)
        if h > 0:
            finish_core(h - 1)

    share = seq // NX
    for xb in range(NX):
        at = slice(xb * share, (xb + 1) * share)
        total = mm(gkv[0, at], w[0])
        for h in range(1, heads):
            total = total + mm(gkv[h, at], w[h])
        gl_send[xb] = total.astype(bf16)

    finish_core(heads - 1)

    def x_copy(k):
        return remote(
            gl_send.at[(my_x + k) % NX], x_recv.at[k - 1], x_ss.at[k - 1], x_rs.at[k - 1], at_x(k)
        )

    for k in (2, 1, 3):
        c = x_copy(k)
        c.start()
        sent.append(c)

    high, low = split(basis[...])
    b_hi[...] = high
    b_lo[...] = low
    per = rows // (NY * NZ * NC)
    for i in range(per):
        at = slice(i * heads, (i + 1) * heads)
        t_fm[at] = fm[i]
        t_sr[at] = sr[i]
        t_sp[at] = sp[i]
    near = pl.multiple_of((dp // 4) * 16, 16)
    o = iota((16, 1), 0)
    old = jnp.zeros((16, latw), f32)
    for h in range(heads):
        pick = jnp.where((o & 3) == h, (dp % 4) * 4 + (o >> 2), -1)
        old = old + mm(one_hot_rows(pick, 16), w[h, pl.ds(near, 16), :])

    for h in range(heads):
        total = z_send[h, my_z].astype(f32)
        for k in range(1, NZ):
            z_copy(h, k).wait_recv()
            total = total + z_recv[h, k - 1].astype(f32)
        bsrc[h * 32 : (h + 1) * 32] = total.astype(bf16)
    o = iota((heads * 32, 1), 0)
    order = one_hot_rows((o & 3) * 32 + (o >> 4) * 4 + ((o >> 2) & 3), heads * 32)
    yb_send[...] = mm(order, bsrc[...]).astype(bf16).reshape(NY, 16, half)

    def yb_copy(k):
        return remote(
            yb_send.at[(my_y + k) % NY], yb_recv.at[k - 1], yb_ss.at[k - 1], yb_rs.at[k - 1], at_y(k)
        )

    for k in (4, 3, 5, 2, 6, 1, 7):
        go_on(yb_copy(k))

    for h in range(heads):
        total = y_send[h, my_y].astype(f32)
        for k in range(1, NY):
            y_copy(h, k).wait_recv()
            total = total + y_recv[h, k - 1].astype(f32)
        asrc[h * 16 : (h + 1) * 16] = total.astype(bf16)
    o = iota((heads * 16, 1), 0)
    order = one_hot_rows((o & 3) * 16 + (o >> 4) * 4 + ((o >> 2) & 3), heads * 16)
    za_send[...] = mm(order, asrc[...]).astype(bf16).reshape(NZ, 16, half)

    def za_copy(k):
        return remote(
            za_send.at[(my_z + k) % NZ], za_recv.at[k - 1], za_ss.at[k - 1], za_rs.at[k - 1], at_z(k)
        )

    for k in (2, 1, 3):
        go_on(za_copy(k))

    total = gl_send[my_x].astype(f32)
    for k in range(1, NX):
        x_copy(k).wait_recv()
        total = total + x_recv[k - 1].astype(f32)
    zh_send[...] = total.astype(bf16).reshape(NH, share // NH, latw)

    def h_copy(k):
        return remote(
            zh_send.at[(my_h + k) % NH], zh_recv.at[k - 1], h_ss.at[k - 1], h_rs.at[k - 1], at_h(k)
        )

    for k in range(1, NH):
        c = h_copy(k)
        c.start()
        sent.append(c)

    lower = za_send[my_z].astype(f32)
    for k in range(1, NZ):
        za_copy(k).wait_recv()
        lower = lower + za_recv[k - 1].astype(f32)
    upper = yb_send[my_y].astype(f32)
    for k in range(1, NY):
        yb_copy(k).wait_recv()
        upper = upper + yb_recv[k - 1].astype(f32)
    grad = jnp.concatenate([lower, upper], axis=1)

    g_hi, g_lo = split(grad)
    rotated = mm(g_hi, b_hi[...]) + mm(g_lo, b_hi[...]) + mm(g_hi, b_lo[...])
    first = beta_first * t_fm[...] + (1.0 - beta_first) * rotated
    second = beta_second * t_sr[...] + (1.0 - beta_second) * rotated * rotated
    plain = beta_second * t_sp[...] + (1.0 - beta_second) * grad * grad
    stacked = jnp.concatenate([first / (jnp.sqrt(second) + epsilon), first], axis=0)
    s_hi, s_lo = split(stacked)
    back = mm(s_hi, b_hi[...], NT) + mm(s_lo, b_hi[...], NT) + mm(s_hi, b_lo[...], NT)
    direction = blend_share * back[:16] + blend_share * back[16:] / (jnp.sqrt(plain) + epsilon)
    new = (old - learn_rate * (direction + decay_rate * old)).astype(bf16)
    for i in range(per):
        gw[my_y, my_z, my_c, i] = new[i * heads : (i + 1) * heads]

    lo, hi = slice(0, per // 2), slice(per // 2, per)

    def y_of(j):
        return (my_y + NY - j) % NY

    def z_of(j):
        return (my_z + NZ - j) % NZ

    def a1(k):
        ref = gw.at[my_y, my_z, my_c, lo]
        return remote(ref, ref, a1_ss.at[k - 1], a1_rs.at[k - 1], at_z(k))

    def b1(k):
        ref = gw.at[my_y, my_z, my_c, hi]
        return remote(ref, ref, b1_ss.at[k - 1], b1_rs.at[k - 1], at_y(k))

    def a2(j, k):
        ref = gw.at[my_y, z_of(j), my_c, lo]
        return remote(ref, ref, a2_ss.at[j, k - 1], a2_rs.at[j, k - 1], at_y(k))

    def b2(j, k):
        ref = gw.at[y_of(j), my_z, my_c, hi]
        return remote(ref, ref, b2_ss.at[j, k - 1], b2_rs.at[j, k - 1], at_z(k))

    def ga(k):
        ref = gw.at[y_of(k), :, my_c, lo]
        return remote(ref, ref, ga_ss.at[k], ga_rs.at[k], partner)

    def gb(k):
        ref = gw.at[:, z_of(k), my_c, hi]
        return remote(ref, ref, gb_ss.at[k], gb_rs.at[k], partner)

    far_y = (4, 3, 5, 2, 6, 1, 7)
    far_z = (2, 1, 3)
    for k in far_z:
        go_on(a1(k))
    for k in far_y:
        go_on(b1(k))
    for k in far_y:
        go_on(a2(0, k))
    for k in far_z:
        go_on(b2(0, k))

    for i in range(per):
        at = slice(i * heads, (i + 1) * heads)
        nf_out[i] = first[at]
        ns_out[i] = second[at]
        np_out[i] = plain[at]

    for side, j in (("y", 1), ("y", 7), ("z", 1), ("z", 3), ("y", 2), ("y", 6), ("z", 2), ("y", 3), ("y", 5), ("y", 4)):
        if side == "y":
            b1(j).wait_recv()
            for k in far_z:
                go_on(b2(j, k))
        else:
            a1(j).wait_recv()
            for k in far_y:
                go_on(a2(j, k))
    go_on(ga(0))
    go_on(gb(0))

    for side, k in (("y", 1), ("y", 7), ("z", 1), ("y", 2), ("y", 6), ("z", 3), ("y", 3), ("y", 5), ("z", 2), ("y", 4)):
        if side == "y":
            for j in range(NZ):
                a2(j, k).wait_recv()
            go_on(ga(k))
        else:
            for j in range(NY):
                b2(j, k).wait_recv()
            go_on(gb(k))
    for k in range(NY):
        ga(k).wait_recv()
    for k in range(NZ):
        gb(k).wait_recv()

    total = zh_send[my_h].astype(f32)
    for k in range(1, NH):
        h_copy(k).wait_recv()
        total = total + zh_recv[k - 1].astype(f32)
    gl_out[...] = total.astype(bf16)
    for c in sent:
        c.wait_send()


def local(
    latent, q_nope, q_rope, k_rope, grad_out, offsets, weight, basis,
    first_moment, second_rot, second_plain,
):
    seq, latw = latent.shape
    rows, heads, _ = weight.shape
    per = first_moment.shape[0]
    by_head = jnp.transpose(weight, (1, 0, 2))
    vmem = pl.BlockSpec(memory_space=pltpu.VMEM)
    dma = pltpu.SemaphoreType.DMA
    V = pltpu.VMEM
    share = seq // NX
    outs = pl.pallas_call(
        kernel,
        out_shape=(
            jax.ShapeDtypeStruct((share // NH, latw), bf16),
            jax.ShapeDtypeStruct((NY, NZ, NC, per, heads, latw), bf16),
            jax.ShapeDtypeStruct((per, heads, latw), f32),
            jax.ShapeDtypeStruct((per, heads, latw), f32),
            jax.ShapeDtypeStruct((per, heads, latw), f32),
        ),
        in_specs=[pl.BlockSpec(memory_space=pltpu.SMEM)] + [vmem] * 10,
        out_specs=[vmem] * 5,
        scratch_shapes=[
            V((2, seq, 128), bf16),
            V((heads, seq, rows), bf16),
            V((2, seq, seq), bf16),
            V((2, seq, seq), bf16),
            V((heads, 2, rows // 2, latw // 2), f32),
            V((heads, 2, rows // 2, latw // 2), bf16),
            V((heads, 2, rows // 2, latw // 2), bf16),
            V((heads, NY, 16, latw // 2), bf16),
            V((heads, NY - 1, 16, latw // 2), bf16),
            V((heads, NZ, 32, latw // 2), bf16),
            V((heads, NZ - 1, 32, latw // 2), bf16),
            V((heads * 16, latw // 2), bf16),
            V((heads * 32, latw // 2), bf16),
            V((NZ, 16, latw // 2), bf16),
            V((NZ - 1, 16, latw // 2), bf16),
            V((NY, 16, latw // 2), bf16),
            V((NY - 1, 16, latw // 2), bf16),
            V((NX, share, latw), bf16),
            V((NX - 1, share, latw), bf16),
            V((NH, share // NH, latw), bf16),
            V((NH - 1, share // NH, latw), bf16),
            V((latw, latw), bf16),
            V((latw, latw), bf16),
            V((16, latw), f32),
            V((16, latw), f32),
            V((16, latw), f32),
            dma((heads,)), dma((heads,)),
            dma((heads, NY - 1)), dma((heads, NY - 1)),
            dma((heads, NZ - 1)), dma((heads, NZ - 1)),
            dma((NZ - 1,)), dma((NZ - 1,)),
            dma((NY - 1,)), dma((NY - 1,)),
            dma((NX - 1,)), dma((NX - 1,)),
            dma((NH - 1,)), dma((NH - 1,)),
            dma((NZ - 1,)), dma((NZ - 1,)),
            dma((NY - 1,)), dma((NY - 1,)),
            dma((NZ, NY - 1)), dma((NZ, NY - 1)),
            dma((NY, NZ - 1)), dma((NY, NZ - 1)),
            dma((NY,)), dma((NY,)),
            dma((NZ,)), dma((NZ,)),
        ],
        compiler_params=pltpu.CompilerParams(
            collective_id=0, has_side_effects=True, vmem_limit_bytes=60 * 2**20
        ),
    )(
        offsets, latent, q_nope, q_rope, k_rope.T, grad_out, by_head, basis,
        first_moment, second_rot, second_plain,
    )
    grad_latent, gathered, moment, rotated_sq, plain_sq = outs
    return (grad_latent, gathered.reshape(rows, heads, latw), moment, rotated_sq, plain_sq)


def solution(mesh):
    return jax.shard_map(
        local,
        mesh=mesh,
        in_specs=(
            P("dp", None),
            P("dp", "tensor"),
            P("dp", "tensor"),
            P("dp", None),
            P("dp", "tensor"),
            P("dp"),
            P(None, "tensor", None),
            P(),
            P("dp", "tensor", None),
            P("dp", "tensor", None),
            P("dp", "tensor", None),
        ),
        out_specs=(
            P(("dp", "tensor"), None),
            P(None, "tensor", None),
            P("dp", "tensor", None),
            P("dp", "tensor", None),
            P("dp", "tensor", None),
        ),
        check_vma=False,
    )
```

```python
import functools
import math

import jax
import jax.numpy as jnp
from jax import lax
from jax.experimental import pallas as pl
from jax.experimental.pallas import tpu as pltpu
from jax.sharding import PartitionSpec as P

beta_first = 0.9
beta_second = 0.95
epsilon = 1e-08
learn_rate = 0.002
decay_rate = 0.1
blend_share = 0.5

NY, NZ, NC = 8, 4, 2
NX, NH = 4, 3
f32 = jnp.float32
bf16 = jnp.bfloat16

NN = (((1,), (0,)), ((), ()))
NT = (((1,), (1,)), ((), ()))
TN = (((0,), (0,)), ((), ()))


def mm(a, b, dims=NN):
    return lax.dot_general(a, b, dims, preferred_element_type=f32)


def iota(shape, dim):
    return lax.broadcasted_iota(jnp.int32, shape, dim)


def one_hot_rows(source, columns):
    return jnp.where(source == iota((source.shape[0], columns), 1), 1.0, 0.0).astype(bf16)


def split(x):
    high = x.astype(bf16)
    return high, (x - high.astype(f32)).astype(bf16)


def kernel(
    off, lat_in, qn_in, qr_in, kr_in, go_in, w_in, basis_in, fm_in, sr_in, sp_in,
    gl_out, gw, nf_out, ns_out, np_out,
    lat, w_raw, kr, qn, qr, go, basis, fm, sr, sp, in_sem, w, krp, gkv, pts, gss, wg_own, wg_send, c_recv, y_send, y_recv, z_send, z_recv,
    asrc, bsrc, za_send, za_recv, yb_send, yb_recv,
    gl_send, x1_recv, x2_send, x2_recv, zh_send, zh_recv, b_hi, b_lo, t_fm, t_sr, t_sp,
    c_ss, c_rs, y_ss, y_rs, z_ss, z_rs, za_ss, za_rs, yb_ss, yb_rs, x1_ss, x1_rs, x2_ss, x2_rs, h_ss, h_rs,
    a1_ss, a1_rs, b1_ss, b1_rs, a2_ss, a2_rs, b2_ss, b2_rs, ga_ss, ga_rs, gb_ss, gb_rs,
):
    loads = {
        name: pltpu.make_async_copy(src, dst, in_sem.at[i])
        for i, (name, src, dst) in enumerate(
            (
                ("lat", lat_in, lat), ("w", w_in, w_raw), ("kr", kr_in, kr), ("qn", qn_in, qn),
                ("qr", qr_in, qr), ("go", go_in, go), ("basis", basis_in, basis),
                ("fm", fm_in, fm), ("sr", sr_in, sr), ("sp", sp_in, sp),
            )
        )
    }
    for load in loads.values():
        load.start()
    seq, _ = lat.shape
    heads, rows, latw = w.shape
    hd = rows // 2
    half = latw // 2
    dp = lax.axis_index("dp")
    tn = lax.axis_index("tensor")
    my_y, my_z, my_c = dp // (NZ * NC), (dp // NC) % NZ, dp % NC
    my_x, my_h = tn // NH, tn % NH

    def at_y(k):
        return (((my_y + k) % NY) * (NZ * NC) + my_z * NC + my_c, tn)

    def at_z(k):
        return (my_y * (NZ * NC) + ((my_z + k) % NZ) * NC + my_c, tn)

    x_near = my_x + 1 - 2 * (my_x % 2)
    x_far = NX - 1 - my_x
    x_to = ((x_near, NX - 1 - x_near), (x_far, x_far + 1 - 2 * (x_far % 2)))

    def at_x(x):
        return (dp, x * NH + my_h)

    def at_h(k):
        return (dp, my_x * NH + (my_h + k) % NH)

    partner = (my_y * (NZ * NC) + my_z * NC + (1 - my_c), tn)

    def remote(src, dst, ss, rs, to):
        return pltpu.make_async_remote_copy(
            src_ref=src, dst_ref=dst, send_sem=ss, recv_sem=rs,
            device_id=to, device_id_type=pl.DeviceIdType.MESH,
        )

    barrier = pltpu.get_barrier_semaphore()
    greet = (
        [partner]
        + [at_y(k) for k in range(1, NY)]
        + [at_z(k) for k in range(1, NZ)]
        + [at_x(x_near), at_x(x_far)]
        + [at_h(k) for k in range(1, NH)]
    )
    for to in greet:
        pl.semaphore_signal(barrier, inc=1, device_id=to, device_id_type=pl.DeviceIdType.MESH)

    sent = []

    loads["kr"].wait()
    rope = kr.shape[0]
    lane = iota((rope, 2 * rope), 1)
    row = iota((rope, 2 * rope), 0)
    for odd in range(2):
        place = jnp.where(lane == row + odd * rope, 1.0, 0.0).astype(bf16)
        krp[odd] = mm(kr[...], place, TN).astype(bf16)

    o = iota((rows, 1), 0)
    core_i = jnp.where((o >> 7) == 0, my_c, 1 - my_c) * 4 + (o & 3)
    perm_a = one_hot_rows(((o >> 4) & 7) * 32 + ((o >> 2) & 3) * 8 + core_i, rows)
    perm_b = one_hot_rows(((o >> 2) & 7) * 32 + ((o >> 5) & 3) * 8 + core_i, rows)

    scale = float(hd + rope) ** (-0.5)
    to_exp2 = scale * math.log2(math.e)
    last_seen = off[0] - 1
    blocks = [(0, 256), (256, 256), (512, seq - 512)]

    def core_copy(h):
        return remote(wg_send.at[h], c_recv.at[h], c_ss.at[h], c_rs.at[h], partner)

    def y_copy(h, k):
        return remote(
            y_send.at[h, (my_y + k) % NY], y_recv.at[h, k - 1],
            y_ss.at[h, k - 1], y_rs.at[h, k - 1], at_y(k),
        )

    def z_copy(h, k):
        return remote(
            z_send.at[h, (my_z + k) % NZ], z_recv.at[h, k - 1],
            z_ss.at[h, k - 1], z_rs.at[h, k - 1], at_z(k),
        )

    def go_on(c):
        c.start()
        sent.append(c)

    def finish_core(h):
        core_copy(h).wait_recv()
        both = (wg_own[h, 0] + c_recv[h, 0].astype(f32)).astype(bf16)
        y_send[h] = both.reshape(NY, 16, half)
        both = (wg_own[h, 1] + c_recv[h, 1].astype(f32)).astype(bf16)
        z_send[h] = both.reshape(NZ, 32, half)
        for k in (4, 3, 5, 2, 6, 1, 7):
            go_on(y_copy(h, k))
        for k in (2, 1, 3):
            go_on(z_copy(h, k))

    loads["lat"].wait()
    loads["w"].wait()
    w[...] = pltpu.einshape("rhc->hrc", w_raw[...])
    for h in range(heads):
        lanes = slice(h * hd, (h + 1) * hd)
        pair = slice((h // 2) * hd, (h // 2 + 1) * hd)
        kv = mm(lat[...], w[h], NT).astype(bf16)
        key = jnp.concatenate([kv[:, :hd], krp[h % 2]], axis=1)
        value = kv[:, hd:]
        buf = h % 2
        if h == 0:
            for name in ("qn", "qr", "go"):
                loads[name].wait()
        for start, size in blocks:
            at = slice(start, start + size)
            query = jnp.concatenate([qn[at, lanes], qr[at, pair]], axis=1)
            scores = mm(key, query, NT)
            limit = jnp.maximum(iota((1, size), 1) + start, last_seen)
            seen = iota((seq, size), 0) <= limit
            masked = jnp.where(seen, scores, -jnp.inf)
            top = jnp.max(masked, axis=0, keepdims=True)
            terms = jnp.exp2((masked - top) * to_exp2)
            probs = terms * (1.0 / jnp.sum(terms, axis=0, keepdims=True))
            low = probs.astype(bf16)
            pts[buf, :, at] = low
            grad_probs = mm(value, go[at, lanes], NT)
            delta = jnp.sum(low.astype(f32) * grad_probs, axis=0, keepdims=True)
            gss[buf, :, at] = (probs * (grad_probs - delta) * scale).astype(bf16)
        grad_keys = mm(gss[buf], qn[:, lanes])
        grad_values = mm(pts[buf], go[:, lanes])
        both = jnp.concatenate([grad_keys.astype(bf16), grad_values.astype(bf16)], axis=1)
        gkv[h] = both
        for side, perm in ((0, perm_a), (1, perm_b)):
            turned = mm(perm, both, NT).astype(bf16)
            part = mm(turned, lat[:, side * half : (side + 1) * half])
            wg_own[h, side] = part[: rows // 2]
            wg_send[h, side] = part[rows // 2 :].astype(bf16)
        if h == 0:
            pl.semaphore_wait(barrier, len(greet))
        c = core_copy(h)
        c.start()
        sent.append(c)
        if h > 0:
            finish_core(h - 1)

    share = seq // NX
    for xb in range(NX):
        at = slice(xb * share, (xb + 1) * share)
        total = mm(gkv[0, at], w[0])
        for h in range(1, heads):
            total = total + mm(gkv[h, at], w[h])
        gl_send[0, xb] = total[:, :half].astype(bf16)
        gl_send[1, xb] = total[:, half:].astype(bf16)

    def x1_copy(side, slot):
        return remote(
            gl_send.at[side, x_to[side][slot]], x1_recv.at[side, slot],
            x1_ss.at[side, slot], x1_rs.at[side, slot], at_x(x_to[side][0]),
        )

    def x2_copy(side):
        return remote(
            x2_send.at[side], x2_recv.at[side], x2_ss.at[side], x2_rs.at[side], at_x(x_to[1 - side][0])
        )

    for slot in (1, 0):
        for side in range(2):
            go_on(x1_copy(side, slot))

    finish_core(heads - 1)

    for side in range(2):
        x1_copy(side, 1).wait_recv()
        total = gl_send[side, x_to[1 - side][0]].astype(f32) + x1_recv[side, 1].astype(f32)
        x2_send[side] = total.astype(bf16)
        go_on(x2_copy(side))

    for name in ("basis", "fm", "sr", "sp"):
        loads[name].wait()
    high, low = split(basis[...])
    b_hi[...] = high
    b_lo[...] = low
    per = rows // (NY * NZ * NC)
    for i in range(per):
        at = slice(i * heads, (i + 1) * heads)
        t_fm[at] = fm[i]
        t_sr[at] = sr[i]
        t_sp[at] = sp[i]
    near = pl.multiple_of((dp // 4) * 16, 16)
    o = iota((16, 1), 0)
    old = jnp.zeros((16, latw), f32)
    for h in range(heads):
        pick = jnp.where((o & 3) == h, (dp % 4) * 4 + (o >> 2), -1)
        old = old + mm(one_hot_rows(pick, 16), w[h, pl.ds(near, 16), :])

    for h in range(heads):
        total = z_send[h, my_z].astype(f32)
        for k in range(1, NZ):
            z_copy(h, k).wait_recv()
            total = total + z_recv[h, k - 1].astype(f32)
        bsrc[h * 32 : (h + 1) * 32] = total.astype(bf16)
    o = iota((heads * 32, 1), 0)
    order = one_hot_rows((o & 3) * 32 + (o >> 4) * 4 + ((o >> 2) & 3), heads * 32)
    yb_send[...] = mm(order, bsrc[...]).astype(bf16).reshape(NY, 16, half)

    def yb_copy(k):
        return remote(
            yb_send.at[(my_y + k) % NY], yb_recv.at[k - 1], yb_ss.at[k - 1], yb_rs.at[k - 1], at_y(k)
        )

    for k in (4, 3, 5, 2, 6, 1, 7):
        go_on(yb_copy(k))

    for h in range(heads):
        total = y_send[h, my_y].astype(f32)
        for k in range(1, NY):
            y_copy(h, k).wait_recv()
            total = total + y_recv[h, k - 1].astype(f32)
        asrc[h * 16 : (h + 1) * 16] = total.astype(bf16)
    o = iota((heads * 16, 1), 0)
    order = one_hot_rows((o & 3) * 16 + (o >> 4) * 4 + ((o >> 2) & 3), heads * 16)
    za_send[...] = mm(order, asrc[...]).astype(bf16).reshape(NZ, 16, half)

    def za_copy(k):
        return remote(
            za_send.at[(my_z + k) % NZ], za_recv.at[k - 1], za_ss.at[k - 1], za_rs.at[k - 1], at_z(k)
        )

    for k in (2, 1, 3):
        go_on(za_copy(k))

    for side in range(2):
        x1_copy(side, 0).wait_recv()
        x2_copy(side).wait_recv()
        total = (
            gl_send[side, my_x].astype(f32) + x1_recv[side, 0].astype(f32) + x2_recv[side].astype(f32)
        )
        zh_send[:, :, side * half : (side + 1) * half] = total.astype(bf16).reshape(
            NH, share // NH, half
        )

    def h_copy(k):
        return remote(
            zh_send.at[(my_h + k) % NH], zh_recv.at[k - 1], h_ss.at[k - 1], h_rs.at[k - 1], at_h(k)
        )

    for k in range(1, NH):
        c = h_copy(k)
        c.start()
        sent.append(c)

    lower = za_send[my_z].astype(f32)
    for k in range(1, NZ):
        za_copy(k).wait_recv()
        lower = lower + za_recv[k - 1].astype(f32)
    upper = yb_send[my_y].astype(f32)
    for k in range(1, NY):
        yb_copy(k).wait_recv()
        upper = upper + yb_recv[k - 1].astype(f32)
    grad = jnp.concatenate([lower, upper], axis=1)

    g_hi, g_lo = split(grad)
    rotated = mm(g_hi, b_hi[...]) + mm(g_lo, b_hi[...]) + mm(g_hi, b_lo[...])
    first = beta_first * t_fm[...] + (1.0 - beta_first) * rotated
    second = beta_second * t_sr[...] + (1.0 - beta_second) * rotated * rotated
    plain = beta_second * t_sp[...] + (1.0 - beta_second) * grad * grad
    stacked = jnp.concatenate([first / (jnp.sqrt(second) + epsilon), first], axis=0)
    s_hi, s_lo = split(stacked)
    back = mm(s_hi, b_hi[...], NT) + mm(s_lo, b_hi[...], NT) + mm(s_hi, b_lo[...], NT)
    direction = blend_share * back[:16] + blend_share * back[16:] / (jnp.sqrt(plain) + epsilon)
    new = (old - learn_rate * (direction + decay_rate * old)).astype(bf16)
    for i in range(per):
        gw[my_y, my_z, my_c, i] = new[i * heads : (i + 1) * heads]

    lo, hi = slice(0, per // 2), slice(per // 2, per)

    def y_of(j):
        return (my_y + NY - j) % NY

    def z_of(j):
        return (my_z + NZ - j) % NZ

    def a1(k):
        ref = gw.at[my_y, my_z, my_c, lo]
        return remote(ref, ref, a1_ss.at[k - 1], a1_rs.at[k - 1], at_z(k))

    def b1(k):
        ref = gw.at[my_y, my_z, my_c, hi]
        return remote(ref, ref, b1_ss.at[k - 1], b1_rs.at[k - 1], at_y(k))

    def a2(j, k):
        ref = gw.at[my_y, z_of(j), my_c, lo]
        return remote(ref, ref, a2_ss.at[j, k - 1], a2_rs.at[j, k - 1], at_y(k))

    def b2(j, k):
        ref = gw.at[y_of(j), my_z, my_c, hi]
        return remote(ref, ref, b2_ss.at[j, k - 1], b2_rs.at[j, k - 1], at_z(k))

    def ga(k):
        ref = gw.at[y_of(k), :, my_c, lo]
        return remote(ref, ref, ga_ss.at[k], ga_rs.at[k], partner)

    def gb(k):
        ref = gw.at[:, z_of(k), my_c, hi]
        return remote(ref, ref, gb_ss.at[k], gb_rs.at[k], partner)

    far_y = (4, 3, 5, 2, 6, 1, 7)
    far_z = (2, 1, 3)
    for k in far_z:
        go_on(a1(k))
    for k in far_y:
        go_on(b1(k))
    for k in far_y:
        go_on(a2(0, k))
    for k in far_z:
        go_on(b2(0, k))

    for i in range(per):
        at = slice(i * heads, (i + 1) * heads)
        nf_out[i] = first[at]
        ns_out[i] = second[at]
        np_out[i] = plain[at]

    for side, j in (("y", 1), ("y", 7), ("z", 1), ("z", 3), ("y", 2), ("y", 6), ("z", 2), ("y", 3), ("y", 5), ("y", 4)):
        if side == "y":
            b1(j).wait_recv()
            for k in far_z:
                go_on(b2(j, k))
        else:
            a1(j).wait_recv()
            for k in far_y:
                go_on(a2(j, k))
    go_on(ga(0))
    go_on(gb(0))

    for side, k in (("y", 1), ("y", 7), ("z", 1), ("y", 2), ("y", 6), ("z", 3), ("y", 3), ("y", 5), ("z", 2), ("y", 4)):
        if side == "y":
            for j in range(NZ):
                a2(j, k).wait_recv()
            go_on(ga(k))
        else:
            for j in range(NY):
                b2(j, k).wait_recv()
            go_on(gb(k))
    for k in range(NY):
        ga(k).wait_recv()
    for k in range(NZ):
        gb(k).wait_recv()

    total = zh_send[my_h].astype(f32)
    for k in range(1, NH):
        h_copy(k).wait_recv()
        total = total + zh_recv[k - 1].astype(f32)
    gl_out[...] = total.astype(bf16)
    for c in sent:
        c.wait_send()


def hand_over(*refs):
    n = (len(refs) - 2) // 3
    ins, outs, held, in_sem, out_sem = refs[:n], refs[n : 2 * n], refs[2 * n : 3 * n], *refs[3 * n :]
    loads = [pltpu.make_async_copy(ins[i], held[i], in_sem.at[i]) for i in range(n)]
    stores = [pltpu.make_async_copy(held[i], outs[i], out_sem.at[i]) for i in range(n)]
    for i in range(n):
        loads[i].start()
    for i in range(n):
        loads[i].wait()
        stores[i].start()
    for i in range(n):
        stores[i].wait()


def store(*arrays):
    anywhere = pl.BlockSpec(memory_space=pl.ANY)
    sem = pltpu.SemaphoreType.DMA((len(arrays),))
    return pl.pallas_call(
        hand_over,
        out_shape=[jax.ShapeDtypeStruct(a.shape, a.dtype) for a in arrays],
        in_specs=[anywhere] * len(arrays),
        out_specs=[anywhere] * len(arrays),
        scratch_shapes=[pltpu.VMEM(a.shape, a.dtype) for a in arrays] + [sem, sem],
        compiler_params=pltpu.CompilerParams(vmem_limit_bytes=60 * 2**20),
    )(*arrays)


def local(
    latent, q_nope, q_rope, k_rope, grad_out, offsets, weight, basis,
    first_moment, second_rot, second_plain,
):
    seq, latw = latent.shape
    rows, heads, _ = weight.shape
    per = first_moment.shape[0]
    vmem = pl.BlockSpec(memory_space=pltpu.VMEM)
    anywhere = pl.BlockSpec(memory_space=pl.ANY)
    dma = pltpu.SemaphoreType.DMA
    V = pltpu.VMEM
    share = seq // NX
    outs = pl.pallas_call(
        kernel,
        out_shape=(
            jax.ShapeDtypeStruct((share // NH, latw), bf16),
            jax.ShapeDtypeStruct((NY, NZ, NC, per, heads, latw), bf16),
            jax.ShapeDtypeStruct((per, heads, latw), f32),
            jax.ShapeDtypeStruct((per, heads, latw), f32),
            jax.ShapeDtypeStruct((per, heads, latw), f32),
        ),
        in_specs=[pl.BlockSpec(memory_space=pltpu.SMEM)] + [anywhere] * 10,
        out_specs=[vmem] * 5,
        scratch_shapes=[
            V(latent.shape, bf16), V(weight.shape, bf16), V(k_rope.shape[::-1], bf16),
            V(q_nope.shape, bf16), V(q_rope.shape, bf16), V(grad_out.shape, bf16),
            V(basis.shape, f32), V(first_moment.shape, f32), V(first_moment.shape, f32),
            V(first_moment.shape, f32), dma((10,)), V((heads, rows, latw), bf16),
            V((2, seq, 128), bf16),
            V((heads, seq, rows), bf16),
            V((2, seq, seq), bf16),
            V((2, seq, seq), bf16),
            V((heads, 2, rows // 2, latw // 2), f32),
            V((heads, 2, rows // 2, latw // 2), bf16),
            V((heads, 2, rows // 2, latw // 2), bf16),
            V((heads, NY, 16, latw // 2), bf16),
            V((heads, NY - 1, 16, latw // 2), bf16),
            V((heads, NZ, 32, latw // 2), bf16),
            V((heads, NZ - 1, 32, latw // 2), bf16),
            V((heads * 16, latw // 2), bf16),
            V((heads * 32, latw // 2), bf16),
            V((NZ, 16, latw // 2), bf16),
            V((NZ - 1, 16, latw // 2), bf16),
            V((NY, 16, latw // 2), bf16),
            V((NY - 1, 16, latw // 2), bf16),
            V((2, NX, share, latw // 2), bf16),
            V((2, 2, share, latw // 2), bf16),
            V((2, share, latw // 2), bf16),
            V((2, share, latw // 2), bf16),
            V((NH, share // NH, latw), bf16),
            V((NH - 1, share // NH, latw), bf16),
            V((latw, latw), bf16),
            V((latw, latw), bf16),
            V((16, latw), f32),
            V((16, latw), f32),
            V((16, latw), f32),
            dma((heads,)), dma((heads,)),
            dma((heads, NY - 1)), dma((heads, NY - 1)),
            dma((heads, NZ - 1)), dma((heads, NZ - 1)),
            dma((NZ - 1,)), dma((NZ - 1,)),
            dma((NY - 1,)), dma((NY - 1,)),
            dma((2, 2)), dma((2, 2)),
            dma((2,)), dma((2,)),
            dma((NH - 1,)), dma((NH - 1,)),
            dma((NZ - 1,)), dma((NZ - 1,)),
            dma((NY - 1,)), dma((NY - 1,)),
            dma((NZ, NY - 1)), dma((NZ, NY - 1)),
            dma((NY, NZ - 1)), dma((NY, NZ - 1)),
            dma((NY,)), dma((NY,)),
            dma((NZ,)), dma((NZ,)),
        ],
        compiler_params=pltpu.CompilerParams(
            collective_id=0, has_side_effects=True, vmem_limit_bytes=60 * 2**20
        ),
    )(
        offsets, latent, q_nope, q_rope, k_rope.T, grad_out, weight, basis,
        first_moment, second_rot, second_plain,
    )
    return store(outs[0], outs[1].reshape(rows, heads, latw), *outs[2:])


def solution(mesh):
    return jax.shard_map(
        local,
        mesh=mesh,
        in_specs=(
            P("dp", None),
            P("dp", "tensor"),
            P("dp", "tensor"),
            P("dp", None),
            P("dp", "tensor"),
            P("dp"),
            P(None, "tensor", None),
            P(),
            P("dp", "tensor", None),
            P("dp", "tensor", None),
            P("dp", "tensor", None),
        ),
        out_specs=(
            P(("dp", "tensor"), None),
            P(None, "tensor", None),
            P("dp", "tensor", None),
            P("dp", "tensor", None),
            P("dp", "tensor", None),
        ),
        check_vma=False,
    )
```

```python
import functools
import math

import jax
import jax.numpy as jnp
from jax import lax
from jax.experimental import pallas as pl
from jax.experimental.pallas import tpu as pltpu
from jax.sharding import PartitionSpec as P

beta_first = 0.9
beta_second = 0.95
epsilon = 1e-08
learn_rate = 0.002
decay_rate = 0.1
blend_share = 0.5

NY, NZ, NC = 8, 4, 2
NX, NH = 4, 3
f32 = jnp.float32
bf16 = jnp.bfloat16

NN = (((1,), (0,)), ((), ()))
NT = (((1,), (1,)), ((), ()))
TN = (((0,), (0,)), ((), ()))


def mm(a, b, dims=NN):
    return lax.dot_general(a, b, dims, preferred_element_type=f32)


def iota(shape, dim):
    return lax.broadcasted_iota(jnp.int32, shape, dim)


def one_hot_rows(source, columns):
    return jnp.where(source == iota((source.shape[0], columns), 1), 1.0, 0.0).astype(bf16)


def split(x):
    high = x.astype(bf16)
    return high, (x - high.astype(f32)).astype(bf16)


def kernel(
    off, lat_in, qn_in, qr_in, kr_in, go_in, w_in, basis_in, fm_in, sr_in, sp_in,
    gl_out, gw, nf_out, ns_out, np_out,
    lat, w_raw, kr, qn, qr, go, basis, fm, sr, sp, in_sem, w, krp, gkv, pts, gss, wg_own, wg_send, c_recv, y_send, y_recv, z_send, z_recv,
    asrc, bsrc, za_send, za_recv, yb_send, yb_recv,
    gl_send, x1_recv, x2_send, x2_recv, zh_send, zh_recv, b_hi, b_lo, t_fm, t_sr, t_sp,
    c_ss, c_rs, y_ss, y_rs, z_ss, z_rs, za_ss, za_rs, yb_ss, yb_rs, x1_ss, x1_rs, x2_ss, x2_rs, h_ss, h_rs,
    a1_ss, a1_rs, b1_ss, b1_rs, a2_ss, a2_rs, b2_ss, b2_rs, ga_ss, ga_rs, gb_ss, gb_rs,
):
    loads = {
        name: pltpu.make_async_copy(src, dst, in_sem.at[i])
        for i, (name, src, dst) in enumerate(
            (
                ("lat", lat_in, lat), ("w", w_in, w_raw), ("kr", kr_in, kr), ("qn", qn_in, qn),
                ("qr", qr_in, qr), ("go", go_in, go), ("basis", basis_in, basis),
                ("fm", fm_in, fm), ("sr", sr_in, sr), ("sp", sp_in, sp),
            )
        )
    }
    for load in loads.values():
        load.start()
    seq, _ = lat.shape
    heads, rows, latw = w.shape
    hd = rows // 2
    half = latw // 2
    dp = lax.axis_index("dp")
    tn = lax.axis_index("tensor")
    my_y, my_z, my_c = dp // (NZ * NC), (dp // NC) % NZ, dp % NC
    my_x, my_h = tn // NH, tn % NH

    def at_y(k):
        return (((my_y + k) % NY) * (NZ * NC) + my_z * NC + my_c, tn)

    def at_z(k):
        return (my_y * (NZ * NC) + ((my_z + k) % NZ) * NC + my_c, tn)

    x_near = my_x + 1 - 2 * (my_x % 2)
    x_far = NX - 1 - my_x
    x_to = ((x_near, NX - 1 - x_near), (x_far, x_far + 1 - 2 * (x_far % 2)))

    def at_x(x):
        return (dp, x * NH + my_h)

    def at_h(k):
        return (dp, my_x * NH + (my_h + k) % NH)

    partner = (my_y * (NZ * NC) + my_z * NC + (1 - my_c), tn)

    def remote(src, dst, ss, rs, to):
        return pltpu.make_async_remote_copy(
            src_ref=src, dst_ref=dst, send_sem=ss, recv_sem=rs,
            device_id=to, device_id_type=pl.DeviceIdType.MESH,
        )

    barrier = pltpu.get_barrier_semaphore()
    greet = (
        [partner]
        + [at_y(k) for k in range(1, NY)]
        + [at_z(k) for k in range(1, NZ)]
        + [at_x(x_near), at_x(x_far)]
        + [at_h(k) for k in range(1, NH)]
    )
    for to in greet:
        pl.semaphore_signal(barrier, inc=1, device_id=to, device_id_type=pl.DeviceIdType.MESH)

    sent = []

    loads["kr"].wait()
    rope = kr.shape[0]
    lane = iota((rope, 2 * rope), 1)
    row = iota((rope, 2 * rope), 0)
    for odd in range(2):
        place = jnp.where(lane == row + odd * rope, 1.0, 0.0).astype(bf16)
        krp[odd] = mm(kr[...], place, TN).astype(bf16)

    o = iota((rows, 1), 0)
    core_i = jnp.where((o >> 7) == 0, my_c, 1 - my_c) * 4 + (o & 3)
    perm_a = one_hot_rows(((o >> 4) & 7) * 32 + ((o >> 2) & 3) * 8 + core_i, rows)
    perm_b = one_hot_rows(((o >> 2) & 7) * 32 + ((o >> 5) & 3) * 8 + core_i, rows)

    scale = float(hd + rope) ** (-0.5)
    to_exp2 = scale * math.log2(math.e)
    last_seen = off[0] - 1
    blocks = [(512, seq - 512), (0, 256), (256, 256)]

    def core_copy(h):
        return remote(wg_send.at[h], c_recv.at[h], c_ss.at[h], c_rs.at[h], partner)

    def y_copy(h, k):
        return remote(
            y_send.at[h, (my_y + k) % NY], y_recv.at[h, k - 1],
            y_ss.at[h, k - 1], y_rs.at[h, k - 1], at_y(k),
        )

    def z_copy(h, k):
        return remote(
            z_send.at[h, (my_z + k) % NZ], z_recv.at[h, k - 1],
            z_ss.at[h, k - 1], z_rs.at[h, k - 1], at_z(k),
        )

    def go_on(c):
        c.start()
        sent.append(c)

    def finish_core(h):
        core_copy(h).wait_recv()
        both = (wg_own[h, 0] + c_recv[h, 0].astype(f32)).astype(bf16)
        y_send[h] = both.reshape(NY, 16, half)
        both = (wg_own[h, 1] + c_recv[h, 1].astype(f32)).astype(bf16)
        z_send[h] = both.reshape(NZ, 32, half)
        for k in (4, 3, 5, 2, 6, 1, 7):
            go_on(y_copy(h, k))
        for k in (2, 1, 3):
            go_on(z_copy(h, k))

    loads["lat"].wait()
    loads["w"].wait()
    w[...] = pltpu.einshape("rhc->hrc", w_raw[...])
    def front(h, start, size, key, value):
        lanes = slice(h * hd, (h + 1) * hd)
        at = slice(start, start + size)
        query = jnp.concatenate([qn[at, lanes], qr[at, (h // 2) * hd : (h // 2 + 1) * hd]], axis=1)
        return mm(key, query, NT), mm(value, go[at, lanes], NT)

    def open_head(h):
        kv = mm(lat[...], w[h], NT).astype(bf16)
        return jnp.concatenate([kv[:, :hd], krp[h % 2]], axis=1), kv[:, hd:]

    steps = [(h, start, size) for h in range(heads) for start, size in blocks]
    key, value = open_head(0)
    for name in ("qn", "qr", "go"):
        loads[name].wait()
    ahead = front(*steps[0], key, value)
    for n, (h, start, size) in enumerate(steps):
        lanes = slice(h * hd, (h + 1) * hd)
        buf = h % 2
        scores, grad_probs = ahead
        if n + 1 < len(steps):
            if steps[n + 1][0] != h:
                key, value = open_head(h + 1)
            ahead = front(*steps[n + 1], key, value)
        limit = jnp.maximum(iota((1, size), 1) + start, last_seen)
        seen = iota((seq, size), 0) <= limit
        masked = jnp.where(seen, scores, -jnp.inf)
        top = jnp.max(masked, axis=0, keepdims=True)
        terms = jnp.exp2((masked - top) * to_exp2)
        low = (terms * (1.0 / jnp.sum(terms, axis=0, keepdims=True))).astype(bf16)
        wide = low.astype(f32)
        delta = jnp.sum(wide * grad_probs, axis=0, keepdims=True)
        pts[buf, :, start : start + size] = low
        gss[buf, :, start : start + size] = (wide * (grad_probs - delta)).astype(bf16)
        if (start, size) != blocks[-1]:
            continue
        grad_keys = mm(gss[buf], qn[:, lanes]) * scale
        grad_values = mm(pts[buf], go[:, lanes])
        both = jnp.concatenate([grad_keys.astype(bf16), grad_values.astype(bf16)], axis=1)
        gkv[h] = both
        for side, perm in ((0, perm_a), (1, perm_b)):
            turned = mm(perm, both, NT).astype(bf16)
            part = mm(turned, lat[:, side * half : (side + 1) * half])
            wg_own[h, side] = part[: rows // 2]
            wg_send[h, side] = part[rows // 2 :].astype(bf16)
        if h == 0:
            pl.semaphore_wait(barrier, len(greet))
        c = core_copy(h)
        c.start()
        sent.append(c)
        if h > 0:
            finish_core(h - 1)

    share = seq // NX
    for xb in range(NX):
        at = slice(xb * share, (xb + 1) * share)
        total = mm(gkv[0, at], w[0])
        for h in range(1, heads):
            total = total + mm(gkv[h, at], w[h])
        gl_send[0, xb] = total[:, :half].astype(bf16)
        gl_send[1, xb] = total[:, half:].astype(bf16)

    def x1_copy(side, slot):
        return remote(
            gl_send.at[side, x_to[side][slot]], x1_recv.at[side, slot],
            x1_ss.at[side, slot], x1_rs.at[side, slot], at_x(x_to[side][0]),
        )

    def x2_copy(side):
        return remote(
            x2_send.at[side], x2_recv.at[side], x2_ss.at[side], x2_rs.at[side], at_x(x_to[1 - side][0])
        )

    for slot in (1, 0):
        for side in range(2):
            go_on(x1_copy(side, slot))

    finish_core(heads - 1)

    for side in range(2):
        x1_copy(side, 1).wait_recv()
        total = gl_send[side, x_to[1 - side][0]].astype(f32) + x1_recv[side, 1].astype(f32)
        x2_send[side] = total.astype(bf16)
        go_on(x2_copy(side))

    for name in ("basis", "fm", "sr", "sp"):
        loads[name].wait()
    high, low = split(basis[...])
    b_hi[...] = high
    b_lo[...] = low
    per = rows // (NY * NZ * NC)
    for i in range(per):
        at = slice(i * heads, (i + 1) * heads)
        t_fm[at] = fm[i]
        t_sr[at] = sr[i]
        t_sp[at] = sp[i]
    near = pl.multiple_of((dp // 4) * 16, 16)
    o = iota((16, 1), 0)
    old = jnp.zeros((16, latw), f32)
    for h in range(heads):
        pick = jnp.where((o & 3) == h, (dp % 4) * 4 + (o >> 2), -1)
        old = old + mm(one_hot_rows(pick, 16), w[h, pl.ds(near, 16), :])

    for h in range(heads):
        total = z_send[h, my_z].astype(f32)
        for k in range(1, NZ):
            z_copy(h, k).wait_recv()
            total = total + z_recv[h, k - 1].astype(f32)
        bsrc[h * 32 : (h + 1) * 32] = total.astype(bf16)
    o = iota((heads * 32, 1), 0)
    order = one_hot_rows((o & 3) * 32 + (o >> 4) * 4 + ((o >> 2) & 3), heads * 32)
    yb_send[...] = mm(order, bsrc[...]).astype(bf16).reshape(NY, 16, half)

    def yb_copy(k):
        return remote(
            yb_send.at[(my_y + k) % NY], yb_recv.at[k - 1], yb_ss.at[k - 1], yb_rs.at[k - 1], at_y(k)
        )

    for k in (4, 3, 5, 2, 6, 1, 7):
        go_on(yb_copy(k))

    for h in range(heads):
        total = y_send[h, my_y].astype(f32)
        for k in range(1, NY):
            y_copy(h, k).wait_recv()
            total = total + y_recv[h, k - 1].astype(f32)
        asrc[h * 16 : (h + 1) * 16] = total.astype(bf16)
    o = iota((heads * 16, 1), 0)
    order = one_hot_rows((o & 3) * 16 + (o >> 4) * 4 + ((o >> 2) & 3), heads * 16)
    za_send[...] = mm(order, asrc[...]).astype(bf16).reshape(NZ, 16, half)

    def za_copy(k):
        return remote(
            za_send.at[(my_z + k) % NZ], za_recv.at[k - 1], za_ss.at[k - 1], za_rs.at[k - 1], at_z(k)
        )

    for k in (2, 1, 3):
        go_on(za_copy(k))

    for side in range(2):
        x1_copy(side, 0).wait_recv()
        x2_copy(side).wait_recv()
        total = (
            gl_send[side, my_x].astype(f32) + x1_recv[side, 0].astype(f32) + x2_recv[side].astype(f32)
        )
        zh_send[:, :, side * half : (side + 1) * half] = total.astype(bf16).reshape(
            NH, share // NH, half
        )

    def h_copy(k):
        return remote(
            zh_send.at[(my_h + k) % NH], zh_recv.at[k - 1], h_ss.at[k - 1], h_rs.at[k - 1], at_h(k)
        )

    for k in range(1, NH):
        c = h_copy(k)
        c.start()
        sent.append(c)

    lower = za_send[my_z].astype(f32)
    for k in range(1, NZ):
        za_copy(k).wait_recv()
        lower = lower + za_recv[k - 1].astype(f32)
    upper = yb_send[my_y].astype(f32)
    for k in range(1, NY):
        yb_copy(k).wait_recv()
        upper = upper + yb_recv[k - 1].astype(f32)
    grad = jnp.concatenate([lower, upper], axis=1)

    g_hi, g_lo = split(grad)
    rotated = mm(g_hi, b_hi[...]) + mm(g_lo, b_hi[...]) + mm(g_hi, b_lo[...])
    first = beta_first * t_fm[...] + (1.0 - beta_first) * rotated
    second = beta_second * t_sr[...] + (1.0 - beta_second) * rotated * rotated
    plain = beta_second * t_sp[...] + (1.0 - beta_second) * grad * grad
    stacked = jnp.concatenate([first / (jnp.sqrt(second) + epsilon), first], axis=0)
    s_hi, s_lo = split(stacked)
    back = mm(s_hi, b_hi[...], NT) + mm(s_lo, b_hi[...], NT) + mm(s_hi, b_lo[...], NT)
    direction = blend_share * back[:16] + blend_share * back[16:] / (jnp.sqrt(plain) + epsilon)
    new = (old - learn_rate * (direction + decay_rate * old)).astype(bf16)
    for i in range(per):
        gw[my_y, my_z, my_c, i] = new[i * heads : (i + 1) * heads]

    lo, hi = slice(0, per // 2), slice(per // 2, per)

    def y_of(j):
        return (my_y + NY - j) % NY

    def z_of(j):
        return (my_z + NZ - j) % NZ

    def a1(k):
        ref = gw.at[my_y, my_z, my_c, lo]
        return remote(ref, ref, a1_ss.at[k - 1], a1_rs.at[k - 1], at_z(k))

    def b1(k):
        ref = gw.at[my_y, my_z, my_c, hi]
        return remote(ref, ref, b1_ss.at[k - 1], b1_rs.at[k - 1], at_y(k))

    def a2(j, k):
        ref = gw.at[my_y, z_of(j), my_c, lo]
        return remote(ref, ref, a2_ss.at[j, k - 1], a2_rs.at[j, k - 1], at_y(k))

    def b2(j, k):
        ref = gw.at[y_of(j), my_z, my_c, hi]
        return remote(ref, ref, b2_ss.at[j, k - 1], b2_rs.at[j, k - 1], at_z(k))

    def ga(k):
        ref = gw.at[y_of(k), :, my_c, lo]
        return remote(ref, ref, ga_ss.at[k], ga_rs.at[k], partner)

    def gb(k):
        ref = gw.at[:, z_of(k), my_c, hi]
        return remote(ref, ref, gb_ss.at[k], gb_rs.at[k], partner)

    far_y = (4, 3, 5, 2, 6, 1, 7)
    far_z = (2, 1, 3)
    for k in far_z:
        go_on(a1(k))
    for k in far_y:
        go_on(b1(k))
    for k in far_y:
        go_on(a2(0, k))
    for k in far_z:
        go_on(b2(0, k))

    for i in range(per):
        at = slice(i * heads, (i + 1) * heads)
        nf_out[i] = first[at]
        ns_out[i] = second[at]
        np_out[i] = plain[at]

    for side, j in (("y", 1), ("y", 7), ("z", 1), ("z", 3), ("y", 2), ("y", 6), ("z", 2), ("y", 3), ("y", 5), ("y", 4)):
        if side == "y":
            b1(j).wait_recv()
            for k in far_z:
                go_on(b2(j, k))
        else:
            a1(j).wait_recv()
            for k in far_y:
                go_on(a2(j, k))
    go_on(ga(0))
    go_on(gb(0))

    for side, k in (("y", 1), ("y", 7), ("z", 1), ("y", 2), ("y", 6), ("z", 3), ("y", 3), ("y", 5), ("z", 2), ("y", 4)):
        if side == "y":
            for j in range(NZ):
                a2(j, k).wait_recv()
            go_on(ga(k))
        else:
            for j in range(NY):
                b2(j, k).wait_recv()
            go_on(gb(k))
    for k in range(NY):
        ga(k).wait_recv()
    for k in range(NZ):
        gb(k).wait_recv()

    total = zh_send[my_h].astype(f32)
    for k in range(1, NH):
        h_copy(k).wait_recv()
        total = total + zh_recv[k - 1].astype(f32)
    gl_out[...] = total.astype(bf16)
    for c in sent:
        c.wait_send()


def hand_over(*refs):
    n = (len(refs) - 1) // 2
    stores = [pltpu.make_async_copy(refs[i], refs[n + i], refs[-1].at[i]) for i in range(n)]
    for copy in stores:
        copy.start()
    for copy in stores:
        copy.wait()


def store(*arrays):
    return pl.pallas_call(
        hand_over,
        out_shape=[jax.ShapeDtypeStruct(a.shape, a.dtype) for a in arrays],
        in_specs=[pl.BlockSpec(memory_space=pltpu.VMEM)] * len(arrays),
        out_specs=[pl.BlockSpec(memory_space=pl.ANY)] * len(arrays),
        scratch_shapes=[pltpu.SemaphoreType.DMA((len(arrays),))],
    )(*(pltpu.with_memory_space_constraint(a, pltpu.VMEM) for a in arrays))


def local(
    latent, q_nope, q_rope, k_rope, grad_out, offsets, weight, basis,
    first_moment, second_rot, second_plain,
):
    seq, latw = latent.shape
    rows, heads, _ = weight.shape
    per = first_moment.shape[0]
    vmem = pl.BlockSpec(memory_space=pltpu.VMEM)
    anywhere = pl.BlockSpec(memory_space=pl.ANY)
    dma = pltpu.SemaphoreType.DMA
    V = pltpu.VMEM
    share = seq // NX
    outs = pl.pallas_call(
        kernel,
        out_shape=(
            V((share // NH, latw), bf16),
            V((NY, NZ, NC, per, heads, latw), bf16),
            V((per, heads, latw), f32),
            V((per, heads, latw), f32),
            V((per, heads, latw), f32),
        ),
        in_specs=[pl.BlockSpec(memory_space=pltpu.SMEM)] + [anywhere] * 10,
        out_specs=[vmem] * 5,
        scratch_shapes=[
            V(latent.shape, bf16), V(weight.shape, bf16), V(k_rope.shape[::-1], bf16),
            V(q_nope.shape, bf16), V(q_rope.shape, bf16), V(grad_out.shape, bf16),
            V(basis.shape, f32), V(first_moment.shape, f32), V(first_moment.shape, f32),
            V(first_moment.shape, f32), dma((10,)), V((heads, rows, latw), bf16),
            V((2, seq, 128), bf16),
            V((heads, seq, rows), bf16),
            V((2, seq, seq), bf16),
            V((2, seq, seq), bf16),
            V((heads, 2, rows // 2, latw // 2), f32),
            V((heads, 2, rows // 2, latw // 2), bf16),
            V((heads, 2, rows // 2, latw // 2), bf16),
            V((heads, NY, 16, latw // 2), bf16),
            V((heads, NY - 1, 16, latw // 2), bf16),
            V((heads, NZ, 32, latw // 2), bf16),
            V((heads, NZ - 1, 32, latw // 2), bf16),
            V((heads * 16, latw // 2), bf16),
            V((heads * 32, latw // 2), bf16),
            V((NZ, 16, latw // 2), bf16),
            V((NZ - 1, 16, latw // 2), bf16),
            V((NY, 16, latw // 2), bf16),
            V((NY - 1, 16, latw // 2), bf16),
            V((2, NX, share, latw // 2), bf16),
            V((2, 2, share, latw // 2), bf16),
            V((2, share, latw // 2), bf16),
            V((2, share, latw // 2), bf16),
            V((NH, share // NH, latw), bf16),
            V((NH - 1, share // NH, latw), bf16),
            V((latw, latw), bf16),
            V((latw, latw), bf16),
            V((16, latw), f32),
            V((16, latw), f32),
            V((16, latw), f32),
            dma((heads,)), dma((heads,)),
            dma((heads, NY - 1)), dma((heads, NY - 1)),
            dma((heads, NZ - 1)), dma((heads, NZ - 1)),
            dma((NZ - 1,)), dma((NZ - 1,)),
            dma((NY - 1,)), dma((NY - 1,)),
            dma((2, 2)), dma((2, 2)),
            dma((2,)), dma((2,)),
            dma((NH - 1,)), dma((NH - 1,)),
            dma((NZ - 1,)), dma((NZ - 1,)),
            dma((NY - 1,)), dma((NY - 1,)),
            dma((NZ, NY - 1)), dma((NZ, NY - 1)),
            dma((NY, NZ - 1)), dma((NY, NZ - 1)),
            dma((NY,)), dma((NY,)),
            dma((NZ,)), dma((NZ,)),
        ],
        compiler_params=pltpu.CompilerParams(
            collective_id=0, has_side_effects=True, vmem_limit_bytes=60 * 2**20
        ),
    )(
        offsets, latent, q_nope, q_rope, k_rope.T, grad_out, weight, basis,
        first_moment, second_rot, second_plain,
    )
    outs = store(*outs)
    return (outs[0], outs[1].reshape(rows, heads, latw), *outs[2:])


def solution(mesh):
    return jax.shard_map(
        local,
        mesh=mesh,
        in_specs=(
            P("dp", None),
            P("dp", "tensor"),
            P("dp", "tensor"),
            P("dp", None),
            P("dp", "tensor"),
            P("dp"),
            P(None, "tensor", None),
            P(),
            P("dp", "tensor", None),
            P("dp", "tensor", None),
            P("dp", "tensor", None),
        ),
        out_specs=(
            P(("dp", "tensor"), None),
            P(None, "tensor", None),
            P("dp", "tensor", None),
            P("dp", "tensor", None),
            P("dp", "tensor", None),
        ),
        check_vma=False,
    )
```

```python
import functools
import math

import jax
import jax.numpy as jnp
from jax import lax
from jax.experimental import pallas as pl
from jax.experimental.pallas import tpu as pltpu
from jax.sharding import PartitionSpec as P

beta_first = 0.9
beta_second = 0.95
epsilon = 1e-08
learn_rate = 0.002
decay_rate = 0.1
blend_share = 0.5

NY, NZ, NC = 8, 4, 2
NX, NH = 4, 3
f32 = jnp.float32
bf16 = jnp.bfloat16

NN = (((1,), (0,)), ((), ()))
NT = (((1,), (1,)), ((), ()))
TN = (((0,), (0,)), ((), ()))


def mm(a, b, dims=NN):
    return lax.dot_general(a, b, dims, preferred_element_type=f32)


def iota(shape, dim):
    return lax.broadcasted_iota(jnp.int32, shape, dim)


def one_hot_rows(source, columns):
    return jnp.where(source == iota((source.shape[0], columns), 1), 1.0, 0.0).astype(bf16)


def split(x):
    high = x.astype(bf16)
    return high, (x - high.astype(f32)).astype(bf16)


def kernel(
    off, lat_in, qn_in, qr_in, kr_in, go_in, w_in, basis_in, fm_in, sr_in, sp_in,
    gl_out, gw, nf_out, ns_out, np_out,
    lat, w_raw, kr, qn, qr, go, basis, fm, sr, sp, in_sem, w, krp, gkv, pts, gss, wg_own, wg_send, c_recv, y_send, y_recv, z_send, z_recv,
    asrc, bsrc, za_send, za_recv, yb_send, yb_recv,
    gl_send, x1_recv, x2_send, x2_recv, zh_send, zh_recv, b_hi, b_lo, t_fm, t_sr, t_sp,
    c_ss, c_rs, y_ss, y_rs, z_ss, z_rs, za_ss, za_rs, yb_ss, yb_rs, x1_ss, x1_rs, x2_ss, x2_rs, h_ss, h_rs,
    a1_ss, a1_rs, b1_ss, b1_rs, a2_ss, a2_rs, b2_ss, b2_rs, ga_ss, ga_rs, gb_ss, gb_rs,
):
    loads = {
        name: pltpu.make_async_copy(src, dst, in_sem.at[i])
        for i, (name, src, dst) in enumerate(
            (
                ("lat", lat_in, lat), ("w", w_in, w_raw), ("kr", kr_in, kr), ("qn", qn_in, qn),
                ("qr", qr_in, qr), ("go", go_in, go), ("basis", basis_in, basis),
                ("fm", fm_in, fm), ("sr", sr_in, sr), ("sp", sp_in, sp),
            )
        )
    }
    late = ("basis", "fm", "sr", "sp")
    for name, load in loads.items():
        if name not in late:
            load.start()
    seq, _ = lat.shape
    heads, rows, latw = w.shape
    hd = rows // 2
    half = latw // 2
    dp = lax.axis_index("dp")
    tn = lax.axis_index("tensor")
    my_y, my_z, my_c = dp // (NZ * NC), (dp // NC) % NZ, dp % NC
    my_x, my_h = tn // NH, tn % NH

    def at_y(k):
        return (((my_y + k) % NY) * (NZ * NC) + my_z * NC + my_c, tn)

    def at_z(k):
        return (my_y * (NZ * NC) + ((my_z + k) % NZ) * NC + my_c, tn)

    x_near = my_x + 1 - 2 * (my_x % 2)
    x_far = NX - 1 - my_x
    x_to = ((x_near, NX - 1 - x_near), (x_far, x_far + 1 - 2 * (x_far % 2)))

    def at_x(x):
        return (dp, x * NH + my_h)

    def at_h(k):
        return (dp, my_x * NH + (my_h + k) % NH)

    partner = (my_y * (NZ * NC) + my_z * NC + (1 - my_c), tn)

    def remote(src, dst, ss, rs, to):
        return pltpu.make_async_remote_copy(
            src_ref=src, dst_ref=dst, send_sem=ss, recv_sem=rs,
            device_id=to, device_id_type=pl.DeviceIdType.MESH,
        )

    barrier = pltpu.get_barrier_semaphore()
    greet = (
        [partner]
        + [at_y(k) for k in range(1, NY)]
        + [at_z(k) for k in range(1, NZ)]
        + [at_x(x_near), at_x(x_far)]
        + [at_h(k) for k in range(1, NH)]
    )
    for to in greet:
        pl.semaphore_signal(barrier, inc=1, device_id=to, device_id_type=pl.DeviceIdType.MESH)

    sent = []

    loads["kr"].wait()
    rope = kr.shape[0]
    lane = iota((rope, 2 * rope), 1)
    row = iota((rope, 2 * rope), 0)
    for odd in range(2):
        place = jnp.where(lane == row + odd * rope, 1.0, 0.0).astype(bf16)
        krp[odd] = mm(kr[...], place, TN).astype(bf16)

    o = iota((rows, 1), 0)
    core_i = jnp.where((o >> 7) == 0, my_c, 1 - my_c) * 4 + (o & 3)
    perm_a = one_hot_rows(((o >> 4) & 7) * 32 + ((o >> 2) & 3) * 8 + core_i, rows)
    perm_b = one_hot_rows(((o >> 2) & 7) * 32 + ((o >> 5) & 3) * 8 + core_i, rows)

    scale = float(hd + rope) ** (-0.5)
    to_exp2 = scale * math.log2(math.e)
    last_seen = off[0] - 1
    blocks = [(512, seq - 512), (0, 256), (256, 256)]

    def core_copy(h):
        return remote(wg_send.at[h], c_recv.at[h], c_ss.at[h], c_rs.at[h], partner)

    def y_copy(h, k):
        return remote(
            y_send.at[h, (my_y + k) % NY], y_recv.at[h, k - 1],
            y_ss.at[h, k - 1], y_rs.at[h, k - 1], at_y(k),
        )

    def z_copy(h, k):
        return remote(
            z_send.at[h, (my_z + k) % NZ], z_recv.at[h, k - 1],
            z_ss.at[h, k - 1], z_rs.at[h, k - 1], at_z(k),
        )

    def go_on(c):
        c.start()
        sent.append(c)

    def finish_core(h):
        core_copy(h).wait_recv()
        both = (wg_own[h, 0] + c_recv[h, 0].astype(f32)).astype(bf16)
        y_send[h] = both.reshape(NY, 16, half)
        both = (wg_own[h, 1] + c_recv[h, 1].astype(f32)).astype(bf16)
        z_send[h] = both.reshape(NZ, 32, half)
        for k in (4, 3, 5, 2, 6, 1, 7):
            go_on(y_copy(h, k))
        for k in (2, 1, 3):
            go_on(z_copy(h, k))

    loads["lat"].wait()
    loads["w"].wait()
    w[...] = pltpu.einshape("rhc->hrc", w_raw[...])
    def front(h, start, size, key, value):
        lanes = slice(h * hd, (h + 1) * hd)
        at = slice(start, start + size)
        query = jnp.concatenate([qn[at, lanes], qr[at, (h // 2) * hd : (h // 2 + 1) * hd]], axis=1)
        return mm(key, query, NT), mm(value, go[at, lanes], NT)

    def open_head(h):
        kv = mm(lat[...], w[h], NT).astype(bf16)
        return jnp.concatenate([kv[:, :hd], krp[h % 2]], axis=1), kv[:, hd:]

    steps = [(h, start, size) for h in range(heads) for start, size in blocks]
    key, value = open_head(0)
    for name in ("qn", "qr", "go"):
        loads[name].wait()
    for name in late:
        loads[name].start()
    ahead = front(*steps[0], key, value)
    for n, (h, start, size) in enumerate(steps):
        lanes = slice(h * hd, (h + 1) * hd)
        buf = h % 2
        scores, grad_probs = ahead
        if n + 1 < len(steps):
            if steps[n + 1][0] != h:
                key, value = open_head(h + 1)
            ahead = front(*steps[n + 1], key, value)
        limit = jnp.maximum(iota((1, size), 1) + start, last_seen)
        seen = iota((seq, size), 0) <= limit
        masked = jnp.where(seen, scores, -jnp.inf)
        top = jnp.max(masked, axis=0, keepdims=True)
        terms = jnp.exp2((masked - top) * to_exp2)
        low = (terms * (1.0 / jnp.sum(terms, axis=0, keepdims=True))).astype(bf16)
        wide = low.astype(f32)
        delta = jnp.sum(wide * grad_probs, axis=0, keepdims=True)
        pts[buf, :, start : start + size] = low
        gss[buf, :, start : start + size] = (wide * (grad_probs - delta)).astype(bf16)
        if (start, size) == blocks[1] and h > 0:
            finish_core(h - 1)
        if (start, size) != blocks[-1]:
            continue
        grad_keys = mm(gss[buf], qn[:, lanes]) * scale
        grad_values = mm(pts[buf], go[:, lanes])
        both = jnp.concatenate([grad_keys.astype(bf16), grad_values.astype(bf16)], axis=1)
        gkv[h] = both
        for side, perm in ((0, perm_a), (1, perm_b)):
            turned = mm(perm, both, NT).astype(bf16)
            part = mm(turned, lat[:, side * half : (side + 1) * half])
            wg_own[h, side] = part[: rows // 2]
            wg_send[h, side] = part[rows // 2 :].astype(bf16)
        if h == 0:
            pl.semaphore_wait(barrier, len(greet))
        c = core_copy(h)
        c.start()
        sent.append(c)

    share = seq // NX
    for xb in range(NX):
        at = slice(xb * share, (xb + 1) * share)
        total = mm(gkv[0, at], w[0])
        for h in range(1, heads):
            total = total + mm(gkv[h, at], w[h])
        gl_send[0, xb] = total[:, :half].astype(bf16)
        gl_send[1, xb] = total[:, half:].astype(bf16)

    def x1_copy(side, slot):
        return remote(
            gl_send.at[side, x_to[side][slot]], x1_recv.at[side, slot],
            x1_ss.at[side, slot], x1_rs.at[side, slot], at_x(x_to[side][0]),
        )

    def x2_copy(side):
        return remote(
            x2_send.at[side], x2_recv.at[side], x2_ss.at[side], x2_rs.at[side], at_x(x_to[1 - side][0])
        )

    for slot in (1, 0):
        for side in range(2):
            go_on(x1_copy(side, slot))

    finish_core(heads - 1)

    for side in range(2):
        x1_copy(side, 1).wait_recv()
        total = gl_send[side, x_to[1 - side][0]].astype(f32) + x1_recv[side, 1].astype(f32)
        x2_send[side] = total.astype(bf16)
        go_on(x2_copy(side))

    for name in late:
        loads[name].wait()
    high, low = split(basis[...])
    b_hi[...] = high
    b_lo[...] = low
    per = rows // (NY * NZ * NC)
    for i in range(per):
        at = slice(i * heads, (i + 1) * heads)
        t_fm[at] = fm[i]
        t_sr[at] = sr[i]
        t_sp[at] = sp[i]
    near = pl.multiple_of((dp // 4) * 16, 16)
    o = iota((16, 1), 0)
    old = jnp.zeros((16, latw), f32)
    for h in range(heads):
        pick = jnp.where((o & 3) == h, (dp % 4) * 4 + (o >> 2), -1)
        old = old + mm(one_hot_rows(pick, 16), w[h, pl.ds(near, 16), :])

    for h in range(heads):
        total = z_send[h, my_z].astype(f32)
        for k in range(1, NZ):
            z_copy(h, k).wait_recv()
            total = total + z_recv[h, k - 1].astype(f32)
        bsrc[h * 32 : (h + 1) * 32] = total.astype(bf16)
    o = iota((heads * 32, 1), 0)
    order = one_hot_rows((o & 3) * 32 + (o >> 4) * 4 + ((o >> 2) & 3), heads * 32)
    yb_send[...] = mm(order, bsrc[...]).astype(bf16).reshape(NY, 16, half)

    def yb_copy(k):
        return remote(
            yb_send.at[(my_y + k) % NY], yb_recv.at[k - 1], yb_ss.at[k - 1], yb_rs.at[k - 1], at_y(k)
        )

    for k in (4, 3, 5, 2, 6, 1, 7):
        go_on(yb_copy(k))

    for h in range(heads):
        total = y_send[h, my_y].astype(f32)
        for k in range(1, NY):
            y_copy(h, k).wait_recv()
            total = total + y_recv[h, k - 1].astype(f32)
        asrc[h * 16 : (h + 1) * 16] = total.astype(bf16)
    o = iota((heads * 16, 1), 0)
    order = one_hot_rows((o & 3) * 16 + (o >> 4) * 4 + ((o >> 2) & 3), heads * 16)
    za_send[...] = mm(order, asrc[...]).astype(bf16).reshape(NZ, 16, half)

    def za_copy(k):
        return remote(
            za_send.at[(my_z + k) % NZ], za_recv.at[k - 1], za_ss.at[k - 1], za_rs.at[k - 1], at_z(k)
        )

    for k in (2, 1, 3):
        go_on(za_copy(k))

    for side in range(2):
        x1_copy(side, 0).wait_recv()
        x2_copy(side).wait_recv()
        total = (
            gl_send[side, my_x].astype(f32) + x1_recv[side, 0].astype(f32) + x2_recv[side].astype(f32)
        )
        zh_send[:, :, side * half : (side + 1) * half] = total.astype(bf16).reshape(
            NH, share // NH, half
        )

    def h_copy(k):
        return remote(
            zh_send.at[(my_h + k) % NH], zh_recv.at[k - 1], h_ss.at[k - 1], h_rs.at[k - 1], at_h(k)
        )

    for k in range(1, NH):
        c = h_copy(k)
        c.start()
        sent.append(c)

    lower = za_send[my_z].astype(f32)
    for k in range(1, NZ):
        za_copy(k).wait_recv()
        lower = lower + za_recv[k - 1].astype(f32)
    upper = yb_send[my_y].astype(f32)
    for k in range(1, NY):
        yb_copy(k).wait_recv()
        upper = upper + yb_recv[k - 1].astype(f32)
    grad = jnp.concatenate([lower, upper], axis=1)

    g_hi, g_lo = split(grad)
    rotated = mm(g_hi, b_hi[...]) + mm(g_lo, b_hi[...]) + mm(g_hi, b_lo[...])
    first = beta_first * t_fm[...] + (1.0 - beta_first) * rotated
    second = beta_second * t_sr[...] + (1.0 - beta_second) * rotated * rotated
    plain = beta_second * t_sp[...] + (1.0 - beta_second) * grad * grad
    stacked = jnp.concatenate([first / (jnp.sqrt(second) + epsilon), first], axis=0)
    s_hi, s_lo = split(stacked)
    back = mm(s_hi, b_hi[...], NT) + mm(s_lo, b_hi[...], NT) + mm(s_hi, b_lo[...], NT)
    direction = blend_share * back[:16] + blend_share * back[16:] / (jnp.sqrt(plain) + epsilon)
    new = (old - learn_rate * (direction + decay_rate * old)).astype(bf16)
    for i in range(per):
        gw[my_y, my_z, my_c, i] = new[i * heads : (i + 1) * heads]

    lo, hi = slice(0, per // 2), slice(per // 2, per)

    def y_of(j):
        return (my_y + NY - j) % NY

    def z_of(j):
        return (my_z + NZ - j) % NZ

    def a1(k):
        ref = gw.at[my_y, my_z, my_c, lo]
        return remote(ref, ref, a1_ss.at[k - 1], a1_rs.at[k - 1], at_z(k))

    def along_y(k):
        return (y_of(5), at_y(NY - 1)) if k == 4 else (my_y, at_y(k))

    def b1(k):
        row, to = along_y(k)
        ref = gw.at[row, my_z, my_c, hi]
        return remote(ref, ref, b1_ss.at[k - 1], b1_rs.at[k - 1], to)

    def a2(j, k):
        row, to = along_y(k)
        ref = gw.at[row, z_of(j), my_c, lo]
        return remote(ref, ref, a2_ss.at[j, k - 1], a2_rs.at[j, k - 1], to)

    def b2(j, k):
        ref = gw.at[y_of(j), my_z, my_c, hi]
        return remote(ref, ref, b2_ss.at[j, k - 1], b2_rs.at[j, k - 1], at_z(k))

    def ga(k):
        ref = gw.at[y_of(k), :, my_c, lo]
        return remote(ref, ref, ga_ss.at[k], ga_rs.at[k], partner)

    def gb(k):
        ref = gw.at[:, z_of(k), my_c, hi]
        return remote(ref, ref, gb_ss.at[k], gb_rs.at[k], partner)

    far_y = (5, 3, 6, 2, 7, 1)
    far_z = (2, 1, 3)
    for k in far_z:
        go_on(a1(k))
    for k in far_y:
        go_on(b1(k))
    for k in far_y:
        go_on(a2(0, k))
    for k in far_z:
        go_on(b2(0, k))

    for i in range(per):
        at = slice(i * heads, (i + 1) * heads)
        nf_out[i] = first[at]
        ns_out[i] = second[at]
        np_out[i] = plain[at]

    for side, j in (("y", 1), ("y", 7), ("z", 1), ("z", 3), ("y", 5), ("y", 2), ("y", 6), ("z", 2), ("y", 3), ("y", 4)):
        if side == "y":
            b1(j).wait_recv()
            if j == 5:
                go_on(b1(4))
            for k in far_z:
                go_on(b2(j, k))
        else:
            a1(j).wait_recv()
            for k in far_y:
                go_on(a2(j, k))
    go_on(ga(0))
    go_on(gb(0))

    for side, k in (("y", 5), ("y", 1), ("y", 7), ("z", 1), ("y", 2), ("y", 6), ("z", 3), ("y", 3), ("z", 2), ("y", 4)):
        if side == "y":
            for j in range(NZ):
                a2(j, k).wait_recv()
                if k == 5:
                    go_on(a2(j, 4))
            go_on(ga(k))
        else:
            for j in range(NY):
                b2(j, k).wait_recv()
            go_on(gb(k))
    for k in range(NY):
        ga(k).wait_recv()
    for k in range(NZ):
        gb(k).wait_recv()

    total = zh_send[my_h].astype(f32)
    for k in range(1, NH):
        h_copy(k).wait_recv()
        total = total + zh_recv[k - 1].astype(f32)
    gl_out[...] = total.astype(bf16)
    for c in sent:
        c.wait_send()


def hand_over(*refs):
    n = (len(refs) - 1) // 2
    stores = [pltpu.make_async_copy(refs[i], refs[n + i], refs[-1].at[i]) for i in range(n)]
    for copy in stores:
        copy.start()
    for copy in stores:
        copy.wait()


def store(*arrays):
    return pl.pallas_call(
        hand_over,
        out_shape=[jax.ShapeDtypeStruct(a.shape, a.dtype) for a in arrays],
        in_specs=[pl.BlockSpec(memory_space=pltpu.VMEM)] * len(arrays),
        out_specs=[pl.BlockSpec(memory_space=pl.ANY)] * len(arrays),
        scratch_shapes=[pltpu.SemaphoreType.DMA((len(arrays),))],
    )(*(pltpu.with_memory_space_constraint(a, pltpu.VMEM) for a in arrays))


def local(
    latent, q_nope, q_rope, k_rope, grad_out, offsets, weight, basis,
    first_moment, second_rot, second_plain,
):
    seq, latw = latent.shape
    rows, heads, _ = weight.shape
    per = first_moment.shape[0]
    vmem = pl.BlockSpec(memory_space=pltpu.VMEM)
    anywhere = pl.BlockSpec(memory_space=pl.ANY)
    dma = pltpu.SemaphoreType.DMA
    V = pltpu.VMEM
    share = seq // NX
    outs = pl.pallas_call(
        kernel,
        out_shape=(
            V((share // NH, latw), bf16),
            V((NY, NZ, NC, per, heads, latw), bf16),
            V((per, heads, latw), f32),
            V((per, heads, latw), f32),
            V((per, heads, latw), f32),
        ),
        in_specs=[pl.BlockSpec(memory_space=pltpu.SMEM)] + [anywhere] * 10,
        out_specs=[vmem] * 5,
        scratch_shapes=[
            V(latent.shape, bf16), V(weight.shape, bf16), V(k_rope.shape[::-1], bf16),
            V(q_nope.shape, bf16), V(q_rope.shape, bf16), V(grad_out.shape, bf16),
            V(basis.shape, f32), V(first_moment.shape, f32), V(first_moment.shape, f32),
            V(first_moment.shape, f32), dma((10,)), V((heads, rows, latw), bf16),
            V((2, seq, 128), bf16),
            V((heads, seq, rows), bf16),
            V((2, seq, seq), bf16),
            V((2, seq, seq), bf16),
            V((heads, 2, rows // 2, latw // 2), f32),
            V((heads, 2, rows // 2, latw // 2), bf16),
            V((heads, 2, rows // 2, latw // 2), bf16),
            V((heads, NY, 16, latw // 2), bf16),
            V((heads, NY - 1, 16, latw // 2), bf16),
            V((heads, NZ, 32, latw // 2), bf16),
            V((heads, NZ - 1, 32, latw // 2), bf16),
            V((heads * 16, latw // 2), bf16),
            V((heads * 32, latw // 2), bf16),
            V((NZ, 16, latw // 2), bf16),
            V((NZ - 1, 16, latw // 2), bf16),
            V((NY, 16, latw // 2), bf16),
            V((NY - 1, 16, latw // 2), bf16),
            V((2, NX, share, latw // 2), bf16),
            V((2, 2, share, latw // 2), bf16),
            V((2, share, latw // 2), bf16),
            V((2, share, latw // 2), bf16),
            V((NH, share // NH, latw), bf16),
            V((NH - 1, share // NH, latw), bf16),
            V((latw, latw), bf16),
            V((latw, latw), bf16),
            V((16, latw), f32),
            V((16, latw), f32),
            V((16, latw), f32),
            dma((heads,)), dma((heads,)),
            dma((heads, NY - 1)), dma((heads, NY - 1)),
            dma((heads, NZ - 1)), dma((heads, NZ - 1)),
            dma((NZ - 1,)), dma((NZ - 1,)),
            dma((NY - 1,)), dma((NY - 1,)),
            dma((2, 2)), dma((2, 2)),
            dma((2,)), dma((2,)),
            dma((NH - 1,)), dma((NH - 1,)),
            dma((NZ - 1,)), dma((NZ - 1,)),
            dma((NY - 1,)), dma((NY - 1,)),
            dma((NZ, NY - 1)), dma((NZ, NY - 1)),
            dma((NY, NZ - 1)), dma((NY, NZ - 1)),
            dma((NY,)), dma((NY,)),
            dma((NZ,)), dma((NZ,)),
        ],
        compiler_params=pltpu.CompilerParams(
            collective_id=0, has_side_effects=True, vmem_limit_bytes=60 * 2**20
        ),
    )(
        offsets, latent, q_nope, q_rope, k_rope.T, grad_out, weight, basis,
        first_moment, second_rot, second_plain,
    )
    outs = store(*outs)
    return (outs[0], outs[1].reshape(rows, heads, latw), *outs[2:])


def solution(mesh):
    return jax.shard_map(
        local,
        mesh=mesh,
        in_specs=(
            P("dp", None),
            P("dp", "tensor"),
            P("dp", "tensor"),
            P("dp", None),
            P("dp", "tensor"),
            P("dp"),
            P(None, "tensor", None),
            P(),
            P("dp", "tensor", None),
            P("dp", "tensor", None),
            P("dp", "tensor", None),
        ),
        out_specs=(
            P(("dp", "tensor"), None),
            P(None, "tensor", None),
            P("dp", "tensor", None),
            P("dp", "tensor", None),
            P("dp", "tensor", None),
        ),
        check_vma=False,
    )
```

```python
import functools
import math

import jax
import jax.numpy as jnp
from jax import lax
from jax.experimental import pallas as pl
from jax.experimental.pallas import tpu as pltpu
from jax.sharding import PartitionSpec as P

beta_first = 0.9
beta_second = 0.95
epsilon = 1e-08
learn_rate = 0.002
decay_rate = 0.1
blend_share = 0.5

NY, NZ, NC = 8, 4, 2
NX, NH = 4, 3
f32 = jnp.float32
bf16 = jnp.bfloat16

NN = (((1,), (0,)), ((), ()))
NT = (((1,), (1,)), ((), ()))
TN = (((0,), (0,)), ((), ()))


def mm(a, b, dims=NN):
    return lax.dot_general(a, b, dims, preferred_element_type=f32)


def iota(shape, dim):
    return lax.broadcasted_iota(jnp.int32, shape, dim)


def one_hot_rows(source, columns):
    return jnp.where(source == iota((source.shape[0], columns), 1), 1.0, 0.0).astype(bf16)


def split(x):
    high = x.astype(bf16)
    return high, (x - high.astype(f32)).astype(bf16)


def kernel(
    off, lat_in, qn_in, qr_in, kr_in, go_in, w_in, basis_in, fm_in, sr_in, sp_in,
    gl_out, gw, nf_out, ns_out, np_out,
    lat, w_raw, kr, qn, qr, go, basis, fm, sr, sp, in_sem, w, krp, gkv, pts, gss, wg_own, wg_send, c_recv, y_send, y_recv, z_send, z_recv,
    asrc, bsrc, za_send, za_recv, yb_send, yb_recv,
    gl_send, x1_recv, x2_send, x2_recv, zh_send, zh_recv, b_hi, b_lo, t_fm, t_sr, t_sp,
    c_ss, c_rs, y_ss, y_rs, z_ss, z_rs, za_ss, za_rs, yb_ss, yb_rs, x1_ss, x1_rs, x2_ss, x2_rs, h_ss, h_rs,
    a1_ss, a1_rs, b1_ss, b1_rs, a2_ss, a2_rs, b2_ss, b2_rs, ga_ss, ga_rs, gb_ss, gb_rs,
):
    loads = {
        name: pltpu.make_async_copy(src, dst, in_sem.at[i])
        for i, (name, src, dst) in enumerate(
            (
                ("lat", lat_in, lat), ("w", w_in, w_raw), ("kr", kr_in, kr), ("qn", qn_in, qn),
                ("qr", qr_in, qr), ("go", go_in, go), ("basis", basis_in, basis),
                ("fm", fm_in, fm), ("sr", sr_in, sr), ("sp", sp_in, sp),
            )
        )
    }
    late = ("basis", "fm", "sr", "sp")
    for name, load in loads.items():
        if name not in late:
            load.start()
    seq, _ = lat.shape
    heads, rows, latw = w.shape
    hd = rows // 2
    half = latw // 2
    dp = lax.axis_index("dp")
    tn = lax.axis_index("tensor")
    my_y, my_z, my_c = dp // (NZ * NC), (dp // NC) % NZ, dp % NC
    my_x, my_h = tn // NH, tn % NH

    def at_y(k):
        return (((my_y + k) % NY) * (NZ * NC) + my_z * NC + my_c, tn)

    def at_z(k):
        return (my_y * (NZ * NC) + ((my_z + k) % NZ) * NC + my_c, tn)

    x_near = my_x + 1 - 2 * (my_x % 2)
    x_far = NX - 1 - my_x
    x_to = ((x_near, NX - 1 - x_near), (x_far, x_far + 1 - 2 * (x_far % 2)))

    def at_x(x):
        return (dp, x * NH + my_h)

    def at_h(k):
        return (dp, my_x * NH + (my_h + k) % NH)

    partner = (my_y * (NZ * NC) + my_z * NC + (1 - my_c), tn)

    def remote(src, dst, ss, rs, to):
        return pltpu.make_async_remote_copy(
            src_ref=src, dst_ref=dst, send_sem=ss, recv_sem=rs,
            device_id=to, device_id_type=pl.DeviceIdType.MESH,
        )

    barrier = pltpu.get_barrier_semaphore()
    greet = (
        [partner]
        + [at_y(k) for k in range(1, NY)]
        + [at_z(k) for k in range(1, NZ)]
        + [at_x(x_near), at_x(x_far)]
        + [at_h(k) for k in range(1, NH)]
    )
    for to in greet:
        pl.semaphore_signal(barrier, inc=1, device_id=to, device_id_type=pl.DeviceIdType.MESH)

    sent = []

    loads["kr"].wait()
    rope = kr.shape[0]
    lane = iota((rope, 2 * rope), 1)
    row = iota((rope, 2 * rope), 0)
    for odd in range(2):
        place = jnp.where(lane == row + odd * rope, 1.0, 0.0).astype(bf16)
        krp[odd] = mm(kr[...], place, TN).astype(bf16)

    o = iota((rows, 1), 0)
    core_i = jnp.where((o >> 7) == 0, my_c, 1 - my_c) * 4 + (o & 3)
    perm_a = one_hot_rows(((o >> 4) & 7) * 32 + ((o >> 2) & 3) * 8 + core_i, rows)
    perm_b = one_hot_rows(((o >> 2) & 7) * 32 + ((o >> 5) & 3) * 8 + core_i, rows)

    scale = float(hd + rope) ** (-0.5)
    to_exp2 = scale * math.log2(math.e)
    last_seen = off[0] - 1
    blocks = [(512, seq - 512), (0, 256), (256, 256)]

    def core_copy(h):
        return remote(wg_send.at[h], c_recv.at[h], c_ss.at[h], c_rs.at[h], partner)

    def y_copy(h, k):
        return remote(
            y_send.at[h, (my_y + k) % NY], y_recv.at[h, k - 1],
            y_ss.at[h, k - 1], y_rs.at[h, k - 1], at_y(k),
        )

    def z_copy(h, k):
        return remote(
            z_send.at[h, (my_z + k) % NZ], z_recv.at[h, k - 1],
            z_ss.at[h, k - 1], z_rs.at[h, k - 1], at_z(k),
        )

    def go_on(c):
        c.start()
        sent.append(c)

    def finish_core(h):
        core_copy(h).wait_recv()
        both = (wg_own[h, 0] + c_recv[h, 0].astype(f32)).astype(bf16)
        y_send[h] = both.reshape(NY, 16, half)
        both = (wg_own[h, 1] + c_recv[h, 1].astype(f32)).astype(bf16)
        z_send[h] = both.reshape(NZ, 32, half)
        for k in (4, 3, 5, 2, 6, 1, 7):
            go_on(y_copy(h, k))
        for k in (2, 1, 3):
            go_on(z_copy(h, k))

    loads["lat"].wait()
    loads["w"].wait()
    w[...] = pltpu.einshape("rhc->hrc", w_raw[...])
    def front(h, start, size, key, value):
        lanes = slice(h * hd, (h + 1) * hd)
        at = slice(start, start + size)
        query = jnp.concatenate([qn[at, lanes], qr[at, (h // 2) * hd : (h // 2 + 1) * hd]], axis=1)
        return mm(key, query, NT), mm(value, go[at, lanes], NT)

    def open_head(h):
        kv = mm(lat[...], w[h], NT).astype(bf16)
        return jnp.concatenate([kv[:, :hd], krp[h % 2]], axis=1), kv[:, hd:]

    steps = [(h, start, size) for h in range(heads) for start, size in blocks]
    key, value = open_head(0)
    for name in ("qn", "qr", "go"):
        loads[name].wait()
    for name in late:
        loads[name].start()
    ahead = front(*steps[0], key, value)
    for n, (h, start, size) in enumerate(steps):
        lanes = slice(h * hd, (h + 1) * hd)
        buf = h % 2
        scores, grad_probs = ahead
        if n + 1 < len(steps):
            if steps[n + 1][0] != h:
                key, value = open_head(h + 1)
            ahead = front(*steps[n + 1], key, value)
        limit = jnp.maximum(iota((1, size), 1) + start, last_seen)
        seen = iota((seq, size), 0) <= limit
        masked = jnp.where(seen, scores, -jnp.inf)
        top = jnp.max(masked, axis=0, keepdims=True)
        terms = jnp.exp2((masked - top) * to_exp2)
        low = (terms * (1.0 / jnp.sum(terms, axis=0, keepdims=True))).astype(bf16)
        wide = low.astype(f32)
        delta = jnp.sum(wide * grad_probs, axis=0, keepdims=True)
        pts[buf, :, start : start + size] = low
        gss[buf, :, start : start + size] = (wide * (grad_probs - delta)).astype(bf16)
        if (start, size) != blocks[-1]:
            continue
        grad_keys = mm(gss[buf], qn[:, lanes]) * scale
        grad_values = mm(pts[buf], go[:, lanes])
        both = jnp.concatenate([grad_keys.astype(bf16), grad_values.astype(bf16)], axis=1)
        gkv[h] = both
        for side, perm in ((0, perm_a), (1, perm_b)):
            turned = mm(perm, both, NT).astype(bf16)
            part = mm(turned, lat[:, side * half : (side + 1) * half])
            wg_own[h, side] = part[: rows // 2]
            wg_send[h, side] = part[rows // 2 :].astype(bf16)
        if h == 0:
            pl.semaphore_wait(barrier, len(greet))
        c = core_copy(h)
        c.start()
        sent.append(c)
        if h > 0:
            finish_core(h - 1)

    share = seq // NX
    for xb in range(NX):
        at = slice(xb * share, (xb + 1) * share)
        total = mm(gkv[0, at], w[0])
        for h in range(1, heads):
            total = total + mm(gkv[h, at], w[h])
        gl_send[0, xb] = total[:, :half].astype(bf16)
        gl_send[1, xb] = total[:, half:].astype(bf16)

    def x1_copy(side, slot):
        return remote(
            gl_send.at[side, x_to[side][slot]], x1_recv.at[side, slot],
            x1_ss.at[side, slot], x1_rs.at[side, slot], at_x(x_to[side][0]),
        )

    def x2_copy(side):
        return remote(
            x2_send.at[side], x2_recv.at[side], x2_ss.at[side], x2_rs.at[side], at_x(x_to[1 - side][0])
        )

    for slot in (1, 0):
        for side in range(2):
            go_on(x1_copy(side, slot))

    finish_core(heads - 1)

    for side in range(2):
        x1_copy(side, 1).wait_recv()
        total = gl_send[side, x_to[1 - side][0]].astype(f32) + x1_recv[side, 1].astype(f32)
        x2_send[side] = total.astype(bf16)
        go_on(x2_copy(side))

    for name in late:
        loads[name].wait()
    high, low = split(basis[...])
    b_hi[...] = high
    b_lo[...] = low
    per = rows // (NY * NZ * NC)
    for i in range(per):
        at = slice(i * heads, (i + 1) * heads)
        t_fm[at] = fm[i]
        t_sr[at] = sr[i]
        t_sp[at] = sp[i]
    near = pl.multiple_of((dp // 4) * 16, 16)
    o = iota((16, 1), 0)
    old = jnp.zeros((16, latw), f32)
    for h in range(heads):
        pick = jnp.where((o & 3) == h, (dp % 4) * 4 + (o >> 2), -1)
        old = old + mm(one_hot_rows(pick, 16), w[h, pl.ds(near, 16), :])

    for h in range(heads):
        total = z_send[h, my_z].astype(f32)
        for k in range(1, NZ):
            z_copy(h, k).wait_recv()
            total = total + z_recv[h, k - 1].astype(f32)
        bsrc[h * 32 : (h + 1) * 32] = total.astype(bf16)
    o = iota((heads * 32, 1), 0)
    order = one_hot_rows((o & 3) * 32 + (o >> 4) * 4 + ((o >> 2) & 3), heads * 32)
    yb_send[...] = mm(order, bsrc[...]).astype(bf16).reshape(NY, 16, half)

    def yb_copy(k):
        return remote(
            yb_send.at[(my_y + k) % NY], yb_recv.at[k - 1], yb_ss.at[k - 1], yb_rs.at[k - 1], at_y(k)
        )

    for k in (4, 3, 5, 2, 6, 1, 7):
        go_on(yb_copy(k))

    for h in range(heads):
        total = y_send[h, my_y].astype(f32)
        for k in range(1, NY):
            y_copy(h, k).wait_recv()
            total = total + y_recv[h, k - 1].astype(f32)
        asrc[h * 16 : (h + 1) * 16] = total.astype(bf16)
    o = iota((heads * 16, 1), 0)
    order = one_hot_rows((o & 3) * 16 + (o >> 4) * 4 + ((o >> 2) & 3), heads * 16)
    za_send[...] = mm(order, asrc[...]).astype(bf16).reshape(NZ, 16, half)

    def za_copy(k):
        return remote(
            za_send.at[(my_z + k) % NZ], za_recv.at[k - 1], za_ss.at[k - 1], za_rs.at[k - 1], at_z(k)
        )

    for k in (2, 1, 3):
        go_on(za_copy(k))

    for side in range(2):
        x1_copy(side, 0).wait_recv()
        x2_copy(side).wait_recv()
        total = (
            gl_send[side, my_x].astype(f32) + x1_recv[side, 0].astype(f32) + x2_recv[side].astype(f32)
        )
        zh_send[:, :, side * half : (side + 1) * half] = total.astype(bf16).reshape(
            NH, share // NH, half
        )

    def h_copy(k):
        return remote(
            zh_send.at[(my_h + k) % NH], zh_recv.at[k - 1], h_ss.at[k - 1], h_rs.at[k - 1], at_h(k)
        )

    for k in range(1, NH):
        c = h_copy(k)
        c.start()
        sent.append(c)

    lower = za_send[my_z].astype(f32)
    for k in range(1, NZ):
        za_copy(k).wait_recv()
        lower = lower + za_recv[k - 1].astype(f32)
    upper = yb_send[my_y].astype(f32)
    for k in range(1, NY):
        yb_copy(k).wait_recv()
        upper = upper + yb_recv[k - 1].astype(f32)
    grad = jnp.concatenate([lower, upper], axis=1)

    g_hi, g_lo = split(grad)
    rotated = mm(g_hi, b_hi[...]) + mm(g_lo, b_hi[...]) + mm(g_hi, b_lo[...])
    first = beta_first * t_fm[...] + (1.0 - beta_first) * rotated
    second = beta_second * t_sr[...] + (1.0 - beta_second) * rotated * rotated
    plain = beta_second * t_sp[...] + (1.0 - beta_second) * grad * grad
    stacked = jnp.concatenate([first / (jnp.sqrt(second) + epsilon), first], axis=0)
    s_hi, s_lo = split(stacked)
    back = mm(s_hi, b_hi[...], NT) + mm(s_lo, b_hi[...], NT) + mm(s_hi, b_lo[...], NT)
    direction = blend_share * back[:16] + blend_share * back[16:] / (jnp.sqrt(plain) + epsilon)
    new = (old - learn_rate * (direction + decay_rate * old)).astype(bf16)
    for i in range(per):
        gw[my_y, my_z, my_c, i] = new[i * heads : (i + 1) * heads]

    lo, hi = slice(0, per // 2), slice(per // 2, per)

    def y_of(j):
        return (my_y + NY - j) % NY

    def z_of(j):
        return (my_z + NZ - j) % NZ

    def a1(k):
        ref = gw.at[my_y, my_z, my_c, lo]
        return remote(ref, ref, a1_ss.at[k - 1], a1_rs.at[k - 1], at_z(k))

    def b1(k):
        ref = gw.at[my_y, my_z, my_c, hi]
        return remote(ref, ref, b1_ss.at[k - 1], b1_rs.at[k - 1], at_y(k))

    def a2(j, k):
        ref = gw.at[my_y, z_of(j), my_c, lo]
        return remote(ref, ref, a2_ss.at[j, k - 1], a2_rs.at[j, k - 1], at_y(k))

    def b2(j, k):
        ref = gw.at[y_of(j), my_z, my_c, hi]
        return remote(ref, ref, b2_ss.at[j, k - 1], b2_rs.at[j, k - 1], at_z(k))

    def ga(k):
        ref = gw.at[y_of(k), :, my_c, lo]
        return remote(ref, ref, ga_ss.at[k], ga_rs.at[k], partner)

    def gb(k):
        ref = gw.at[:, z_of(k), my_c, hi]
        return remote(ref, ref, gb_ss.at[k], gb_rs.at[k], partner)

    far_y = (4, 3, 5, 2, 6, 1, 7)
    far_z = (2, 1, 3)
    for k in far_z:
        go_on(a1(k))
    for k in far_y:
        go_on(b1(k))
    for k in far_y:
        go_on(a2(0, k))
    for k in far_z:
        go_on(b2(0, k))

    for i in range(per):
        at = slice(i * heads, (i + 1) * heads)
        nf_out[i] = first[at]
        ns_out[i] = second[at]
        np_out[i] = plain[at]

    for side, j in (("y", 1), ("y", 7), ("z", 1), ("z", 3), ("y", 2), ("y", 6), ("z", 2), ("y", 3), ("y", 5), ("y", 4)):
        if side == "y":
            b1(j).wait_recv()
            for k in far_z:
                go_on(b2(j, k))
        else:
            a1(j).wait_recv()
            for k in far_y:
                go_on(a2(j, k))
    go_on(ga(0))
    go_on(gb(0))

    for side, k in (("y", 1), ("y", 7), ("z", 1), ("y", 2), ("y", 6), ("z", 3), ("y", 3), ("y", 5), ("z", 2), ("y", 4)):
        if side == "y":
            for j in range(NZ):
                a2(j, k).wait_recv()
            go_on(ga(k))
        else:
            for j in range(NY):
                b2(j, k).wait_recv()
            go_on(gb(k))
    for k in range(NY):
        ga(k).wait_recv()
    for k in range(NZ):
        gb(k).wait_recv()

    total = zh_send[my_h].astype(f32)
    for k in range(1, NH):
        h_copy(k).wait_recv()
        total = total + zh_recv[k - 1].astype(f32)
    gl_out[...] = total.astype(bf16)
    for c in sent:
        c.wait_send()


def hand_over(*refs):
    n = (len(refs) - 1) // 2
    stores = [pltpu.make_async_copy(refs[i], refs[n + i], refs[-1].at[i]) for i in range(n)]
    for copy in stores:
        copy.start()
    for copy in stores:
        copy.wait()


def store(*arrays):
    return pl.pallas_call(
        hand_over,
        out_shape=[jax.ShapeDtypeStruct(a.shape, a.dtype) for a in arrays],
        in_specs=[pl.BlockSpec(memory_space=pltpu.VMEM)] * len(arrays),
        out_specs=[pl.BlockSpec(memory_space=pl.ANY)] * len(arrays),
        scratch_shapes=[pltpu.SemaphoreType.DMA((len(arrays),))],
    )(*(pltpu.with_memory_space_constraint(a, pltpu.VMEM) for a in arrays))


def local(
    latent, q_nope, q_rope, k_rope, grad_out, offsets, weight, basis,
    first_moment, second_rot, second_plain,
):
    seq, latw = latent.shape
    rows, heads, _ = weight.shape
    per = first_moment.shape[0]
    vmem = pl.BlockSpec(memory_space=pltpu.VMEM)
    anywhere = pl.BlockSpec(memory_space=pl.ANY)
    dma = pltpu.SemaphoreType.DMA
    V = pltpu.VMEM
    share = seq // NX
    outs = pl.pallas_call(
        kernel,
        out_shape=(
            V((share // NH, latw), bf16),
            V((NY, NZ, NC, per, heads, latw), bf16),
            V((per, heads, latw), f32),
            V((per, heads, latw), f32),
            V((per, heads, latw), f32),
        ),
        in_specs=[pl.BlockSpec(memory_space=pltpu.SMEM)] + [anywhere] * 10,
        out_specs=[vmem] * 5,
        scratch_shapes=[
            V(latent.shape, bf16), V(weight.shape, bf16), V(k_rope.shape[::-1], bf16),
            V(q_nope.shape, bf16), V(q_rope.shape, bf16), V(grad_out.shape, bf16),
            V(basis.shape, f32), V(first_moment.shape, f32), V(first_moment.shape, f32),
            V(first_moment.shape, f32), dma((10,)), V((heads, rows, latw), bf16),
            V((2, seq, 128), bf16),
            V((heads, seq, rows), bf16),
            V((2, seq, seq), bf16),
            V((2, seq, seq), bf16),
            V((heads, 2, rows // 2, latw // 2), f32),
            V((heads, 2, rows // 2, latw // 2), bf16),
            V((heads, 2, rows // 2, latw // 2), bf16),
            V((heads, NY, 16, latw // 2), bf16),
            V((heads, NY - 1, 16, latw // 2), bf16),
            V((heads, NZ, 32, latw // 2), bf16),
            V((heads, NZ - 1, 32, latw // 2), bf16),
            V((heads * 16, latw // 2), bf16),
            V((heads * 32, latw // 2), bf16),
            V((NZ, 16, latw // 2), bf16),
            V((NZ - 1, 16, latw // 2), bf16),
            V((NY, 16, latw // 2), bf16),
            V((NY - 1, 16, latw // 2), bf16),
            V((2, NX, share, latw // 2), bf16),
            V((2, 2, share, latw // 2), bf16),
            V((2, share, latw // 2), bf16),
            V((2, share, latw // 2), bf16),
            V((NH, share // NH, latw), bf16),
            V((NH - 1, share // NH, latw), bf16),
            V((latw, latw), bf16),
            V((latw, latw), bf16),
            V((16, latw), f32),
            V((16, latw), f32),
            V((16, latw), f32),
            dma((heads,)), dma((heads,)),
            dma((heads, NY - 1)), dma((heads, NY - 1)),
            dma((heads, NZ - 1)), dma((heads, NZ - 1)),
            dma((NZ - 1,)), dma((NZ - 1,)),
            dma((NY - 1,)), dma((NY - 1,)),
            dma((2, 2)), dma((2, 2)),
            dma((2,)), dma((2,)),
            dma((NH - 1,)), dma((NH - 1,)),
            dma((NZ - 1,)), dma((NZ - 1,)),
            dma((NY - 1,)), dma((NY - 1,)),
            dma((NZ, NY - 1)), dma((NZ, NY - 1)),
            dma((NY, NZ - 1)), dma((NY, NZ - 1)),
            dma((NY,)), dma((NY,)),
            dma((NZ,)), dma((NZ,)),
        ],
        compiler_params=pltpu.CompilerParams(
            collective_id=0, has_side_effects=True, vmem_limit_bytes=60 * 2**20
        ),
    )(
        offsets, latent, q_nope, q_rope, k_rope.T, grad_out, weight, basis,
        first_moment, second_rot, second_plain,
    )
    outs = store(*outs)
    return (outs[0], outs[1].reshape(rows, heads, latw), *outs[2:])


def solution(mesh):
    return jax.shard_map(
        local,
        mesh=mesh,
        in_specs=(
            P("dp", None),
            P("dp", "tensor"),
            P("dp", "tensor"),
            P("dp", None),
            P("dp", "tensor"),
            P("dp"),
            P(None, "tensor", None),
            P(),
            P("dp", "tensor", None),
            P("dp", "tensor", None),
            P("dp", "tensor", None),
        ),
        out_specs=(
            P(("dp", "tensor"), None),
            P(None, "tensor", None),
            P("dp", "tensor", None),
            P("dp", "tensor", None),
            P("dp", "tensor", None),
        ),
        check_vma=False,
    )
```
